128 devices in a mesh: row: 16 (over x, y_lo, core), col: 8 (over y_hi, z).
Axes of the slice: x: 4, y: 4 (y_hi: 2, y_lo: 2; y = y_hi * 2 + y_lo), z: 4, core: 2. Of those that a mesh axis runs over, the one named last changes fastest.
Arguments:
- hidden_states: bfloat16 [16384, 2048], P('row', 'col'), may hold values from -21 to 21
- lengths: int32 [32], P('row'), may hold values from 16 to 512, as said below
- qkvg_master: float32 [2048, 12288], P(('row', 'col')), may hold values from -0.125 to 0.125
- gateup_master: float32 [2, 2048, 4096], P(None, ('row', 'col')), may hold values from -0.125 to 0.125
- out_master: float32 [4096, 2048], P(None, ('row', 'col')), may hold values from -0.09375 to 0.09375
- down_master: float32 [4096, 2048], P(None, ('row', 'col')), may hold values from -0.09375 to 0.09375
Outputs:
- layer_output: bfloat16 [16384, 2048], P('row', 'col')
- qkvg_weight: bfloat16 [2048, 12288], P('row', 'col')
- gateup_weight: bfloat16 [2, 2048, 4096], P(None, 'row', 'col')
- mixing_weight: bfloat16 [4096, 2048], P('col', 'row')
- down_weight: bfloat16 [4096, 2048], P('col', 'row')
The draws below stay inside these ranges and needn't reach their ends.
Inputs may be any that keep to these rules, and one draw needn't show every extreme that they name: `lengths`: prompt length of each request; the positions of a request from its length on are padding. Some request has length 512 in every draw.
All inputs are finite; a program needn't handle non-finite values.
Results may differ from the reference program's by a relative error of at most 0.014.
Values may be sent and summed in bfloat16 or wider, within the bound.
A program may use at most 128 MiB of HBM per device.

```python
import math
import jax
import jax.numpy as jnp
from jax import lax

D = 2048
HEADS = 8
KEY = 256
VAL = 512
FF = 4096
S = 512
BLOCK = 256
REQ = 32
TOKENS = 16384
N_COL = 8


def draw_hidden_states(key, part):
    first_key, second_key = jax.random.split(key, 2)
    column_scale = jnp.exp(jax.random.uniform(first_key, (D,), jnp.float32, math.log(0.3), math.log(3.0)))
    values = jnp.clip(jax.random.normal(second_key, (TOKENS, D), jnp.float32), -6.0, 6.0) * column_scale[None, :]
    return values.astype(jnp.bfloat16)


def draw_lengths(key, part):
    first_key, second_key, third_key = jax.random.split(key, 3)
    short = jax.random.randint(first_key, (REQ,), 16, min(65, S))
    coin = jax.random.randint(second_key, (REQ,), 0, 20)
    chosen = jax.random.randint(third_key, (), 0, REQ)
    longer = (coin < 7) | (jnp.arange(REQ) == chosen)
    return jnp.where(longer, S, short).astype(jnp.int32)


def steps_of(own_key, extent, shards, smallest, high):
    factor_of, own = 1.0, jax.random.fold_in(own_key, 6)
    for dim, shards_of in shards:
        draws = jnp.exp(jax.random.uniform(jax.random.fold_in(own, dim), (shards_of,), jnp.float32, smallest / len(shards), high / len(shards)))
        factor_of = factor_of * jnp.repeat(draws, extent[dim] // shards_of).reshape([-1 if axis == dim else 1 for axis in range(len(extent))])
    return factor_of


def bell_draw(rng, dims, scale, most, cuts=(), kind=jnp.bfloat16):
    values = scale * jax.random.normal(rng, dims, jnp.float32)
    if cuts:
        values = values * steps_of(rng, dims, cuts, -0.22, 0.18)
    return jnp.clip(values, -most, most).astype(kind)


def setup_inputs(seed: int = 0) -> dict:
    keys = jax.random.split(jax.random.key(seed), 7)
    return {
        "hidden_states": draw_hidden_states(jax.random.fold_in(keys[6], 71), 0),
        "lengths": draw_lengths(jax.random.fold_in(keys[6], 71), 0),
        "qkvg_master": bell_draw(keys[2], (D, HEADS * (2 * KEY + 2 * VAL)), D ** -0.5, 0.125, ((0, 128),), jnp.float32),
        "gateup_master": bell_draw(keys[3], (2, D, FF), D ** -0.5, 0.125, ((1, 128),), jnp.float32),
        "out_master": bell_draw(keys[4], (HEADS * VAL, D), (HEADS * VAL) ** -0.5, 0.09375, ((1, 128),), jnp.float32),
        "down_master": bell_draw(keys[5], (FF, D), FF ** -0.5, 0.09375, ((1, 128),), jnp.float32),
    }


epsilon = 1e-05

def to_half(values):
    return lax.optimization_barrier(values.astype(jnp.bfloat16))

def rms_round(values):
    scale = lax.rsqrt(lax.optimization_barrier(jnp.mean(values * values, axis=-1, keepdims=True)) + epsilon)
    return to_half(values * scale)

def rotate(values, positions):
    half = values.shape[-1] // 2
    freq = jnp.power(10000.0, -2.0 * jnp.arange(half).astype(jnp.float32) / values.shape[-1])
    angle = positions.astype(jnp.float32)[:, None] * freq[None, :]
    cosine = jnp.cos(angle)[:, None, :]
    sine = jnp.sin(angle)[:, None, :]
    first = values[..., :half]
    second = values[..., half:]
    return jnp.concatenate([first * cosine - second * sine, first * sine + second * cosine], axis=-1)

def retain(gammas, query, keyed, value):
    heads = query.shape[1]
    blocks = S // BLOCK
    offsets = jnp.arange(BLOCK)
    lag = offsets[:, None] - offsets[None, :]
    within = jnp.where((lag >= 0)[None], jnp.power(gammas[:, None, None], jnp.maximum(lag, 0).astype(jnp.float32)[None]), 0.0)
    into = jnp.power(gammas[:, None], (offsets + 1).astype(jnp.float32)[None, :])
    leaving = jnp.power(gammas[:, None], (BLOCK - 1 - offsets).astype(jnp.float32)[None, :])
    across_blocks_sum = jnp.power(gammas, 1.0 * BLOCK)
    upper_bound = lax.Precision.HIGHEST

    def advance(carry, inputs):
        retention_state, key_sum = carry
        query_block, key_block, value_tile_rows = inputs
        query_float = query_block.astype(jnp.float32)
        key_float = key_block.astype(jnp.float32)
        value_single_float = value_tile_rows.astype(jnp.float32)
        scores = jnp.einsum('thk,shk->hts', query_float, key_float, precision=upper_bound) * within
        denom_inside = lax.optimization_barrier(jnp.sum(scores, axis=2))
        weights = to_half(scores).astype(jnp.float32)
        inside = jnp.einsum('hts,shv->thv', weights, value_single_float, precision=upper_bound)
        damped_query_rows = query_float * jnp.transpose(into)[:, :, None]
        carried_state = jnp.einsum('swc,wcm->swm', damped_query_rows, retention_state, precision=upper_bound)
        denom_carried = jnp.einsum('thk,hk->th', damped_query_rows, key_sum, precision=upper_bound)
        damped_key_rows = key_float * jnp.transpose(leaving)[:, :, None]
        retention_state = across_blocks_sum[:, None, None] * retention_state + jnp.einsum('wat,wag->atg', damped_key_rows, value_single_float, precision=upper_bound)
        key_sum = across_blocks_sum[:, None] * key_sum + lax.optimization_barrier(jnp.sum(damped_key_rows, axis=0))
        denom = jnp.transpose(denom_inside) + denom_carried
        result = (inside + carried_state) / jnp.maximum(jnp.abs(denom), 1.0)[:, :, None]
        return ((retention_state, key_sum), result)
    start = (jnp.zeros((heads, KEY, VAL), jnp.float32), jnp.zeros((heads, KEY), jnp.float32))
    sliced = (query.reshape(blocks, BLOCK, heads, KEY), keyed.reshape(blocks, BLOCK, heads, KEY), value.reshape(blocks, BLOCK, heads, VAL))
    _, results = lax.scan(advance, start, sliced)
    return results.reshape(S, heads, VAL)

def gate_heads(retained, gate):
    centre = lax.optimization_barrier(jnp.mean(retained, axis=-1, keepdims=True))
    centred = retained - centre
    spread = lax.optimization_barrier(jnp.mean(centred * centred, axis=-1, keepdims=True))
    grouped = centred * lax.rsqrt(spread + epsilon)
    return to_half(jax.nn.silu(gate.astype(jnp.float32)) * grouped)

def group_sum(left, right):
    width = left.shape[1] // N_COL
    terms = jnp.einsum('tcv,cvd->ctd', left.astype(jnp.float32).reshape(left.shape[0], N_COL, width), right.astype(jnp.float32).reshape(N_COL, width, right.shape[1]), precision=lax.Precision.HIGHEST)
    return lax.optimization_barrier(jnp.sum(to_half(terms).astype(jnp.float32), axis=0))

def request_layer(inputs, qkvg_weight, gateup_weight, mixing_weight, down_weight):
    tokens, length = inputs
    normed = rms_round(tokens.astype(jnp.float32))
    projected = to_half(jnp.dot(normed, qkvg_weight, preferred_element_type=jnp.float32)).reshape(S, HEADS, 2 * KEY + 2 * VAL)
    positions = jnp.arange(S)
    query = to_half(rotate(projected[:, :, :KEY].astype(jnp.float32), positions))
    keyed = to_half(rotate(projected[:, :, KEY:2 * KEY].astype(jnp.float32), positions) * (1.0 / math.sqrt(KEY)))
    value = projected[:, :, 2 * KEY:2 * KEY + VAL]
    gate = projected[:, :, 2 * KEY + VAL:]
    gammas = 1.0 - jnp.power(2.0, -5.0 - jnp.arange(HEADS).astype(jnp.float32))
    retained = retain(gammas, query, keyed, value)
    mixed = gate_heads(retained, gate).reshape(S, HEADS * VAL)
    residual = tokens.astype(jnp.float32) + group_sum(mixed, mixing_weight)
    normed_mid = rms_round(residual)
    gate_part = jnp.dot(normed_mid, gateup_weight[0], preferred_element_type=jnp.float32)
    up_part = jnp.dot(normed_mid, gateup_weight[1], preferred_element_type=jnp.float32)
    hidden = to_half(jax.nn.silu(gate_part) * up_part)
    feed = group_sum(hidden, down_weight)
    live = positions < length
    return jnp.where(live[:, None], residual + feed, 0.0).astype(jnp.bfloat16)

def reference(hidden_states, lengths, qkvg_master, gateup_master, out_master, down_master):
    qkvg_weight = qkvg_master.astype(jnp.bfloat16)
    gateup_weight = gateup_master.astype(jnp.bfloat16)
    mixing_weight = out_master.astype(jnp.bfloat16)
    down_weight = down_master.astype(jnp.bfloat16)

    def one_request(inputs):
        return request_layer(inputs, qkvg_weight, gateup_weight, mixing_weight, down_weight)
    outputs = lax.map(one_request, (hidden_states.reshape(REQ, S, D), lengths))
    return (outputs.reshape(TOKENS, D), qkvg_weight, gateup_weight, mixing_weight, down_weight)
```

```python
import math

import jax
import jax.numpy as jnp
import numpy as np
from jax import lax
from jax.experimental import pallas as pl
from jax.experimental.pallas import tpu as pltpu
from jax.sharding import PartitionSpec as P

D = 2048
HEADS = 8
KEY = 256
VAL = 512
S = 512
BLOCK = 256
FF = 4096
WIDE = 2 * KEY + 2 * VAL
TOK = 1024
FEAT = 256
REQS = 2
EPS = 1e-05
MESH = pl.DeviceIdType.MESH
BF = jnp.bfloat16
F32 = jnp.float32
NT = (((1,), (1,)), ((), ()))


def tables():
    half = KEY // 2
    freq = np.power(np.float32(10000.0), (-2.0 * np.arange(half) / KEY).astype(np.float32))
    angle = np.arange(S, dtype=np.float32)[:, None] * freq.astype(np.float32)[None, :]
    return np.cos(angle).astype(np.float32), np.sin(angle).astype(np.float32)


def kernel(
    hid, qm, gm, om, dm, cosr, sinr,
    y, oq, of, oo,
    sbq, sbo, sbf, srvq, srvo, srvf,
    xg, xm, gq, go, gf, acc, scl, near, far, qs, ks, mixed, hidden,
    part, pairs, relay, final, resid, outb, swapb,
    send_sem, sem_a2a, sem_own, sem_w, sem_x, sem_core, sem_rel, sem_fin, sem_swap, loc_sem,
):
    row = lax.axis_index("row")
    col = lax.axis_index("col")
    x = lax.div(row, 4)
    u = lax.rem(lax.div(row, 2), 2)
    c = lax.rem(row, 2)
    h = lax.div(col, 4)
    z = lax.rem(col, 4)
    v = 1 - u
    xp, xn, xo = lax.rem(x + 1, 4), lax.rem(x + 3, 4), lax.rem(x + 2, 4)
    zp, zn, zo = lax.rem(z + 1, 4), lax.rem(z + 3, 4), lax.rem(z + 2, 4)
    source = c == h

    def device(xx, uu, cc, hh, zz):
        return (xx * 4 + uu * 2 + cc, hh * 4 + zz)

    to_core = device(x, u, 1 - c, h, z)
    to_swap = device(x, u, h, c, z)
    to_xp, to_xn = device(xp, u, c, h, z), device(xn, u, c, h, z)
    to_zp, to_zn = device(x, u, c, h, zp), device(x, u, c, h, zn)
    to_ya, to_yb = device(x, v, c, h, z), device(x, v, c, 1 - h, z)

    pending = []
    count = [0]

    def post(build, target, when=None):
        index = count[0]
        count[0] += 1

        def copy():
            src, dst, recv = build()
            return pltpu.make_async_remote_copy(
                src_ref=src,
                dst_ref=dst,
                send_sem=send_sem.at[index],
                recv_sem=recv,
                device_id=target,
                device_id_type=MESH,
            )

        copy().start()
        pending.append((when, copy))

    def arrived(dst, recv):
        pltpu.make_async_remote_copy(
            src_ref=dst,
            dst_ref=dst,
            send_sem=send_sem.at[0],
            recv_sem=recv,
            device_id=to_core,
            device_id_type=MESH,
        ).wait_recv()

    barrier = pltpu.get_barrier_semaphore()
    peers = [(row, lax.rem(col + i, 8)) for i in range(1, 8)]
    swap_peer = device(x, u, 1 - c, 1 - h, z)
    greet = peers + [to_core, swap_peer, to_xp, to_xn, to_ya, to_yb]
    for peer in greet:
        pl.semaphore_signal(barrier, inc=1, device_id=peer, device_id_type=MESH)
    for i in range(8):
        sbq[i] = qm[:, i * WIDE : (i + 1) * WIDE].astype(BF)
    pl.semaphore_wait(barrier, len(greet))

    def exchange(buf, serve, group):
        rows = pl.ds(pl.multiple_of(col * 16, 16), 16)
        for i in range(1, 8):
            other = lax.rem(col + i, 8)
            post(
                lambda i=i, other=other: (
                    buf.at[other], serve.at[rows, :], sem_a2a.at[group * 8 + i]
                ),
                (row, other),
            )
        serve[rows, :] = buf[col]

    def exchanged(serve, group):
        for i in range(1, 8):
            sender = lax.rem(col + 8 - i, 8)
            rows = pl.ds(pl.multiple_of(sender * 16, 16), 16)
            arrived(serve.at[rows, :], sem_a2a.at[group * 8 + i])

    exchange(sbq, srvq, 0)

    def lanes(slot):
        return pl.ds(pl.multiple_of(slot * FEAT, FEAT), FEAT)

    mine = c * 4 + z

    def start_swap():
        @pl.when(jnp.logical_not(source))
        def _():
            post(lambda: (hid, xg.at[:, lanes(col)], sem_swap.at[0]), to_swap, "receiver")

        @pl.when(source)
        def _():
            xg[:, lanes(col)] = hid[...]

    start_swap()

    for i in range(8):
        sbo[i] = om[:, i * VAL : (i + 1) * VAL].astype(BF)
        sbf[i, :, 0:512] = gm[0, :, i * 512 : (i + 1) * 512].astype(BF)
        sbf[i, :, 512:1024] = gm[1, :, i * 512 : (i + 1) * 512].astype(BF)
        sbf[i, :, 1024:1536] = dm[:, i * 512 : (i + 1) * 512].astype(BF)
    exchange(sbo, srvo, 1)
    exchange(sbf, srvf, 2)

    head = c * 4 + z
    rate = jnp.float32(0.0)
    for i in range(HEADS):
        rate = jnp.where(head == i, jnp.float32(math.log1p(-(2.0 ** (-5 - i)))), rate)
    lag = lax.broadcasted_iota(jnp.int32, (BLOCK, BLOCK), 0) - lax.broadcasted_iota(
        jnp.int32, (BLOCK, BLOCK), 1
    )
    near[...] = jnp.where(lag >= 0, jnp.exp(jnp.maximum(lag, 0).astype(F32) * rate), 0.0)
    far[...] = jnp.exp((lag + BLOCK).astype(F32) * rate)

    def act_ref(buf, rows, slot):
        return buf.at[rows, lanes(slot)]

    def act_post(buf, rows, slot, recv, to):
        post(lambda: (act_ref(buf, rows, slot), act_ref(buf, rows, slot), recv), to)

    def gather_start(buf, first, size, bank):
        rows = pl.ds(first, size)
        for to in (to_zp, to_zn, to_core):
            act_post(buf, rows, mine, sem_x.at[bank * 16 + mine * 2], to)

    def gather_near(buf, first, size, bank):
        rows = pl.ds(first, size)
        half = size // 2
        for zz, start, to, part_id in ((zn, first, to_zp, 0), (zp, first + half, to_zn, 1)):
            slot = c * 4 + zz
            here = act_ref(buf, rows, slot)
            arrived(here, sem_x.at[bank * 16 + slot * 2])
            act_post(buf, pl.ds(start, half), slot, sem_x.at[bank * 16 + slot * 2 + part_id], to)
            act_post(buf, rows, slot, sem_x.at[bank * 16 + slot * 2], to_core)

    def gather_far(buf, first, size, bank):
        rows = pl.ds(first, size)
        half = size // 2
        slot = c * 4 + zo
        for part_id in range(2):
            arrived(
                act_ref(buf, pl.ds(first + part_id * half, half), slot),
                sem_x.at[bank * 16 + slot * 2 + part_id],
            )
        act_post(buf, rows, slot, sem_x.at[bank * 16 + slot * 2], to_core)

    def gather_core(buf, first, size, bank):
        rows = pl.ds(first, size)
        for zz in (z, zn, zp, zo):
            slot = (1 - c) * 4 + zz
            arrived(act_ref(buf, rows, slot), sem_x.at[bank * 16 + slot * 2])

    def weights(buf, serve, bank):
        xs = (x, xn, xp, xo)

        def block(xx, uu, cc, half=None):
            start = (xx * 4 + uu * 2 + cc) * 128
            if half is None:
                return buf.at[pl.ds(pl.multiple_of(start, 128), 128), :]
            return buf.at[pl.ds(pl.multiple_of(start + half * 64, 64), 64), :]

        def mark(xx, uu, cc, half=None):
            return sem_w.at[bank * 32 + (xx * 4 + uu * 2 + cc) * 2 + (half or 0)]

        def send(who, key, to, half=None):
            post(lambda: (block(*key, half), block(*key, half), mark(*key, half)), to, who)

        def wait(key, half=None):
            arrived(block(*key, half), mark(*key, half))

        def own():
            @pl.when(source)
            def _():
                buf[pl.ds(pl.multiple_of(row * 128, 128), 128), :] = serve[...]

            @pl.when(jnp.logical_not(source))
            def _():
                post(lambda: (serve, block(x, u, c), sem_own.at[bank]), to_core, "receiver")

        def start():
            @pl.when(source)
            def _():
                arrived(block(x, u, 1 - c), sem_own.at[bank])
                for cc, order in ((0, (to_xp, to_xn, to_ya, to_yb)), (1, (to_ya, to_yb, to_xp, to_xn))):
                    for to in order:
                        send("source", (x, u, cc), to)

        def early():
            @pl.when(source)
            def _():
                me = "source"
                wait((xn, u, 0))
                send(me, (xn, u, 0), to_xp, 0)
                send(me, (xn, u, 0), to_ya)
                send(me, (xn, u, 0), to_yb)
                wait((xp, u, 0))
                send(me, (xp, u, 0), to_xn, 1)
                send(me, (xp, u, 0), to_ya)
                send(me, (xp, u, 0), to_yb)
                wait((x, v, 1))
                send(me, (x, v, 1), to_yb, 1)
                send(me, (x, v, 1), to_xp)
                send(me, (x, v, 1), to_xn)
                wait((xn, u, 1))
                send(me, (xn, u, 1), to_xp, 0)
                wait((xp, u, 1))
                send(me, (xp, u, 1), to_xn, 1)
                wait((xo, u, 0), 0)
                wait((xo, u, 0), 1)
                send(me, (xo, u, 0), to_ya)
                send(me, (xo, u, 0), to_yb)

            @pl.when(jnp.logical_not(source))
            def _():
                me = "receiver"
                wait((x, v, 1))
                send(me, (x, v, 1), to_ya, 0)
                send(me, (x, v, 1), to_xp)
                send(me, (x, v, 1), to_xn)
                wait((x, v, 0))
                wait((xn, v, 0))
                send(me, (xn, v, 0), to_ya)
                wait((xp, v, 0))
                send(me, (xp, v, 0), to_ya)
                wait((x, u, 1), 0)
                wait((x, u, 1), 1)
                send(me, (x, u, 1), to_xp)
                send(me, (x, u, 1), to_xn)
                wait((xn, v, 1))
                send(me, (xn, v, 1), to_xp, 0)
                wait((xp, v, 1))
                send(me, (xp, v, 1), to_xn, 1)

        def late(i):
            @pl.when(source)
            def _():
                me = "source"
                wait((xs[i], v, 0))
                if i in (0, 3):
                    send(me, (xs[i], v, 0), to_yb)
                if i == 1:
                    wait((xn, v, 1))
                    send(me, (xn, v, 1), to_xp, 0)
                if i == 2:
                    wait((xp, v, 1))
                    send(me, (xp, v, 1), to_xn, 1)
                if i == 3:
                    for uu in (u, v):
                        wait((xo, uu, 1), 0)
                        wait((xo, uu, 1), 1)

            @pl.when(jnp.logical_not(source))
            def _():
                me = "receiver"
                if i == 1:
                    wait((xn, u, 1))
                    send(me, (xn, u, 1), to_xp, 0)
                if i == 2:
                    wait((xp, u, 1))
                    send(me, (xp, u, 1), to_xn, 1)
                wait((xs[i], u, 0))
                if i == 3:
                    wait((xo, v, 0))
                    for uu in (v, u):
                        wait((xo, uu, 1), 0)
                        wait((xo, uu, 1), 1)

        return own, start, early, late

    own_q, start_q, early_q, late_q = weights(gq, srvq, 0)
    own_o, start_o, early_o, late_o = weights(go, srvo, 1)
    own_f, start_f, early_f, late_f = weights(gf, srvf, 2)

    exchanged(srvq, 0)
    own_q()

    @pl.when(jnp.logical_not(source))
    def _():
        arrived(xg.at[:, lanes(mine)], sem_swap.at[0])

    start_q()
    gather_start(xg, 0, TOK, 0)
    exchanged(srvo, 1)
    own_o()
    exchanged(srvf, 2)
    own_f()
    oq[...] = srvq[...]
    oo[...] = srvo[...]
    of[...] = srvf[...]
    early_q()
    gather_near(xg, 0, TOK, 0)
    gather_far(xg, 0, TOK, 0)
    start_o()
    gather_core(xg, 0, TOK, 0)

    def scales(buf, first):
        @pl.loop(0, S // 128)
        def _(i):
            rows = pl.ds(pl.multiple_of(first + i * 128, 128), 128)
            tokens = buf[rows, :].astype(F32)
            total = jnp.sum(tokens * tokens, axis=1, keepdims=True)
            scl[rows, :] = jnp.broadcast_to(lax.rsqrt(total * (1.0 / D) + EPS), (128, 128))

    scales(xg, 0)
    scales(xg, S)

    for i, xx in enumerate((x, xn, xp, xo)):
        late_q(i)
        feats = pl.ds(pl.multiple_of(xx * 512, 512), 512)

        @pl.loop(0, WIDE // 256)
        def _(n):
            wide = pl.ds(pl.multiple_of(n * 256, 256), 256)
            for m in range(REQS):
                rows = pl.ds(m * S, S)
                term = jnp.dot(xg[rows, feats], gq[feats, wide], preferred_element_type=F32)
                if i == 0:
                    acc[rows, wide] = term
                else:
                    acc[rows, wide] += term

    def retention(r):
        first = r * S
        rows = pl.ds(first, S)
        scale = scl[rows, :]
        for ref, at, gain in ((qs, 0, 1.0), (ks, KEY, 1.0 / math.sqrt(KEY))):
            a = (acc[rows, at : at + 128] * scale).astype(BF).astype(F32)
            b = (acc[rows, at + 128 : at + 256] * scale).astype(BF).astype(F32)
            ref[:, 0:128] = ((a * cosr[...] - b * sinr[...]) * gain).astype(BF)
            ref[:, 128:256] = ((a * sinr[...] + b * cosr[...]) * gain).astype(BF)
        wide_scale = jnp.concatenate([scale] * 4, axis=1)
        value = (acc[rows, 512:1024] * wide_scale).astype(BF)
        for t in range(S // BLOCK):
            q = qs[t * BLOCK : (t + 1) * BLOCK, :]
            total = jnp.zeros((BLOCK, VAL), F32)
            denom = jnp.zeros((BLOCK, 1), F32)
            for s in range(t + 1):
                k = ks[s * BLOCK : (s + 1) * BLOCK, :]
                score = lax.dot_general(q, k, NT, preferred_element_type=F32)
                score = score * (near[...] if s == t else far[...])
                denom += jnp.sum(score, axis=1, keepdims=True)
                total += jnp.dot(
                    score.astype(BF),
                    value[s * BLOCK : (s + 1) * BLOCK, :],
                    preferred_element_type=F32,
                )
            kept = total / jnp.maximum(jnp.abs(denom), 1.0)
            centred = kept - jnp.mean(kept, axis=1, keepdims=True)
            spread = jnp.mean(centred * centred, axis=1, keepdims=True)
            block = pl.ds(first + t * BLOCK, BLOCK)
            gate = (acc[block, 1024:1536] * wide_scale[t * BLOCK : (t + 1) * BLOCK, :]).astype(BF)
            mixed[block, :] = (
                jax.nn.silu(gate.astype(F32)) * (centred * lax.rsqrt(spread + EPS))
            ).astype(BF)

    def terms(left, weight, at, r, bank):
        rows = pl.ds(r * S, S)
        base = count[0]
        count[0] += 4
        copies = []

        def term(slot):
            feats = pl.ds(pl.multiple_of(slot * FEAT, FEAT), FEAT)
            part[r, slot] = lax.dot_general(
                left[rows, :], weight[feats, at : at + 512], NT, preferred_element_type=F32
            ).astype(BF)

        def to_other(j):
            zz = lax.rem(zo + j, 4)
            slot = (1 - c) * 4 + zz
            return pltpu.make_async_remote_copy(
                src_ref=part.at[r, slot],
                dst_ref=pairs.at[bank, r, zz],
                send_sem=send_sem.at[base + j],
                recv_sem=sem_core.at[bank * 8 + r * 4 + zz],
                device_id=to_core,
                device_id_type=MESH,
            )

        @pl.loop(0, 4)
        def _(j):
            term((1 - c) * 4 + lax.rem(zo + j, 4))
            to_other(j).start()

        @pl.loop(0, 4)
        def _(j):
            term(c * 4 + lax.rem(zo + j, 4))

        def sent():
            @pl.loop(0, 4)
            def _(j):
                to_other(j).wait_send()

        return sent

    HALF = S // 2
    TOP, BOT = pl.ds(0, HALF), pl.ds(HALF, HALF)

    def pair(r, bank, zz):
        arrived(pairs.at[bank, r, zz], sem_core.at[bank * 8 + r * 4 + zz])
        slot = c * 4 + zz
        return slot

    def both(r, bank, zz, rows):
        return part[r, c * 4 + zz, rows, :].astype(F32) + pairs[bank, r, zz, rows, :].astype(F32)

    def reduce_start(r, bank):
        base = (bank * 2 + r) * 4
        rel = (bank * 2 + r) * 2
        slot = pair(r, bank, zo)
        part[r, slot] = both(r, bank, zo, pl.ds(0, S)).astype(BF)
        post(lambda slot=slot: (part.at[r, slot, TOP, :], relay.at[bank, r, 0], sem_rel.at[rel]), to_zp)
        post(lambda slot=slot: (part.at[r, slot, BOT, :], relay.at[bank, r, 1], sem_rel.at[rel + 1]), to_zn)
        slot = pair(r, bank, zp)
        part[r, slot, BOT, :] = both(r, bank, zp, BOT).astype(BF)
        post(lambda slot=slot: (part.at[r, slot, BOT, :], final.at[bank, r, 0, BOT, :], sem_fin.at[base + 1]), to_zp)
        slot = pair(r, bank, zn)
        part[r, slot, TOP, :] = both(r, bank, zn, TOP).astype(BF)
        post(lambda slot=slot: (part.at[r, slot, TOP, :], final.at[bank, r, 1, TOP, :], sem_fin.at[base + 2]), to_zn)

    def reduce_relay(r, bank):
        base = (bank * 2 + r) * 4
        rel = (bank * 2 + r) * 2
        arrived(relay.at[bank, r, 0], sem_rel.at[rel])
        slot = c * 4 + zp
        part[r, slot, TOP, :] = (both(r, bank, zp, TOP) + relay[bank, r, 0].astype(F32)).astype(BF)
        post(lambda slot=slot: (part.at[r, slot, TOP, :], final.at[bank, r, 0, TOP, :], sem_fin.at[base]), to_zp)
        arrived(relay.at[bank, r, 1], sem_rel.at[rel + 1])
        slot = c * 4 + zn
        part[r, slot, BOT, :] = (both(r, bank, zn, BOT) + relay[bank, r, 1].astype(F32)).astype(BF)
        post(lambda slot=slot: (part.at[r, slot, BOT, :], final.at[bank, r, 1, BOT, :], sem_fin.at[base + 3]), to_zn)
        pair(r, bank, z)

    def reduce_end(r, bank):
        base = (bank * 2 + r) * 4
        arrived(final.at[bank, r, 0, BOT, :], sem_fin.at[base + 1])
        arrived(final.at[bank, r, 1, TOP, :], sem_fin.at[base + 2])
        arrived(final.at[bank, r, 0, TOP, :], sem_fin.at[base])
        arrived(final.at[bank, r, 1, BOT, :], sem_fin.at[base + 3])
        return (
            both(r, bank, z, pl.ds(0, S))
            + final[bank, r, 0].astype(F32)
            + final[bank, r, 1].astype(F32)
        )

    def add_residual(r):
        rows = pl.ds(r * S, S)
        total = xg[rows, lanes(mine)].astype(F32) + reduce_end(r, 0)
        resid[rows, :] = total
        xm[rows, lanes(mine)] = total.astype(BF)

    def feed(r):
        rows = pl.ds(r * S, S)
        scales(xm, r * S)
        scale = jnp.concatenate([scl[rows, :]] * 2, axis=1)

        @pl.loop(0, 2)
        def _(n):
            at = pl.ds(pl.multiple_of(n * 256, 256), 256)
            up_at = pl.ds(pl.multiple_of(512 + n * 256, 256), 256)
            gate = jnp.dot(xm[rows, :], gf[:, at], preferred_element_type=F32) * scale
            up = jnp.dot(xm[rows, :], gf[:, up_at], preferred_element_type=F32) * scale
            hidden[rows, at] = (jax.nn.silu(gate) * up).astype(BF)

    def finish(r):
        rows = pl.ds(r * S, S)
        outb[rows, :] = (resid[rows, :] + reduce_end(r, 1)).astype(BF)

        @pl.when(jnp.logical_not(source))
        def _():
            post(
                lambda: (outb.at[rows, :], swapb.at[rows, :], sem_swap.at[1 + r]),
                to_swap,
                "receiver",
            )

    retention(0)
    early_o()
    start_f()
    retention(1)
    for i in range(4):
        late_o(i)
    sent = []
    sent.append(terms(mixed, go, 0, 0, 0))
    early_f()
    sent.append(terms(mixed, go, 0, 1, 0))
    reduce_start(0, 0)
    late_f(0)
    reduce_relay(0, 0)
    reduce_start(1, 0)
    late_f(1)
    reduce_relay(1, 0)
    add_residual(0)
    gather_start(xm, 0, S, 1)
    late_f(2)
    add_residual(1)
    gather_start(xm, S, S, 2)
    late_f(3)
    gather_near(xm, 0, S, 1)
    gather_far(xm, 0, S, 1)
    gather_near(xm, S, S, 2)
    gather_core(xm, 0, S, 1)
    feed(0)
    gather_far(xm, S, S, 2)

    for one in sent:
        one()
    for when, copy in pending:
        assert when in (None, "source", "receiver")
    plain = [copy for when, copy in pending if when is None]
    for copy in plain:
        copy().wait_send()
    pending[:] = [(when, copy) for when, copy in pending if when is not None]

    last = [terms(hidden, gf, 1024, 0, 1)]
    gather_core(xm, S, S, 2)
    reduce_start(0, 1)
    feed(1)
    reduce_relay(0, 1)
    last.append(terms(hidden, gf, 1024, 1, 1))
    reduce_start(1, 1)
    finish(0)
    reduce_relay(1, 1)
    finish(1)

    @pl.when(source)
    def _():
        y[...] = outb[...]

    @pl.when(jnp.logical_not(source))
    def _():
        for r in range(REQS):
            rows = pl.ds(r * S, S)
            arrived(swapb.at[rows, :], sem_swap.at[1 + r])
        y[...] = swapb[...]

    for one in last:
        one()
    for when, copy in pending:
        if when is None:
            copy().wait_send()

    @pl.when(source)
    def _():
        for when, copy in pending:
            if when == "source":
                copy().wait_send()

    @pl.when(jnp.logical_not(source))
    def _():
        for when, copy in pending:
            if when == "receiver":
                copy().wait_send()


def layer(hidden, qkvg, gateup, out_t, down_t):
    cosine, sine = tables()
    vmem = pl.BlockSpec(memory_space=pltpu.VMEM)
    dma = pltpu.SemaphoreType.DMA
    scratch = [
        pltpu.VMEM((8, 16, WIDE), BF),
        pltpu.VMEM((8, 16, 512), BF),
        pltpu.VMEM((8, 16, 1536), BF),
        pltpu.VMEM((128, WIDE), BF),
        pltpu.VMEM((128, 512), BF),
        pltpu.VMEM((128, 1536), BF),
        pltpu.VMEM((TOK, D), BF),
        pltpu.VMEM((TOK, D), BF),
        pltpu.VMEM((D, WIDE), BF),
        pltpu.VMEM((D, 512), BF),
        pltpu.VMEM((D, 1536), BF),
        pltpu.VMEM((TOK, WIDE), F32),
        pltpu.VMEM((TOK, 128), F32),
        pltpu.VMEM((BLOCK, BLOCK), F32),
        pltpu.VMEM((BLOCK, BLOCK), F32),
        pltpu.VMEM((S, KEY), BF),
        pltpu.VMEM((S, KEY), BF),
        pltpu.VMEM((TOK, VAL), BF),
        pltpu.VMEM((TOK, 512), BF),
        pltpu.VMEM((REQS, 8, S, FEAT), BF),
        pltpu.VMEM((2, REQS, 4, S, FEAT), BF),
        pltpu.VMEM((2, REQS, 2, S // 2, FEAT), BF),
        pltpu.VMEM((2, REQS, 2, S, FEAT), BF),
        pltpu.VMEM((TOK, FEAT), F32),
        pltpu.VMEM((TOK, FEAT), BF),
        pltpu.VMEM((TOK, FEAT), BF),
        dma((256,)),
        dma((24,)),
        dma((3,)),
        dma((96,)),
        dma((48,)),
        dma((16,)),
        dma((8,)),
        dma((16,)),
        dma((3,)),
        dma((1,)),
    ]
    return pl.pallas_call(
        kernel,
        out_shape=(
            jax.ShapeDtypeStruct((TOK, FEAT), BF),
            jax.ShapeDtypeStruct((128, WIDE), BF),
            jax.ShapeDtypeStruct((128, 1536), BF),
            jax.ShapeDtypeStruct((128, 512), BF),
        ),
        in_specs=[vmem] * 7,
        out_specs=(vmem,) * 4,
        scratch_shapes=scratch,
        compiler_params=pltpu.CompilerParams(
            collective_id=0, has_side_effects=True, vmem_limit_bytes=62 * 1024 * 1024
        ),
    )(hidden, qkvg, gateup, out_t, down_t, jnp.asarray(cosine), jnp.asarray(sine))


def shards(hidden_states, lengths, qkvg_master, gateup_master, out_master, down_master):
    y, wq, wf, wo = layer(
        hidden_states, qkvg_master, gateup_master, out_master.T, down_master.T
    )
    live = jnp.arange(S)[None, :] < lengths[:, None]
    output = jnp.where(live.reshape(TOK, 1), y, jnp.zeros_like(y))
    gateup = jnp.stack([wf[:, 0:512], wf[:, 512:1024]])
    return (output, wq, gateup, wo.T, wf[:, 1024:1536].T)


def solution(mesh):
    return jax.shard_map(
        shards,
        mesh=mesh,
        in_specs=(
            P("row", "col"),
            P("row"),
            P(("row", "col"), None),
            P(None, ("row", "col"), None),
            P(None, ("row", "col")),
            P(None, ("row", "col")),
        ),
        out_specs=(
            P("row", "col"),
            P("row", "col"),
            P(None, "row", "col"),
            P("col", "row"),
            P("col", "row"),
        ),
        check_vma=False,
    )
```

```python
import math

import jax
import jax.numpy as jnp
import numpy as np
from jax import lax
from jax.experimental import pallas as pl
from jax.experimental.pallas import tpu as pltpu
from jax.sharding import PartitionSpec as P

D = 2048
HEADS = 8
KEY = 256
VAL = 512
S = 512
BLOCK = 256
FF = 4096
WIDE = 2 * KEY + 2 * VAL
TOK = 1024
FEAT = 256
REQS = 2
EPS = 1e-05
MESH = pl.DeviceIdType.MESH
BF = jnp.bfloat16
F32 = jnp.float32
NT = (((1,), (1,)), ((), ()))


def tables():
    half = KEY // 2
    freq = np.power(np.float32(10000.0), (-2.0 * np.arange(half) / KEY).astype(np.float32))
    angle = np.arange(S, dtype=np.float32)[:, None] * freq.astype(np.float32)[None, :]
    return np.cos(angle).astype(np.float32), np.sin(angle).astype(np.float32)


def kernel(
    lens, hid, qm_hbm, gm_hbm, om_hbm, dm_hbm, cos_hbm, sin_hbm,
    y, oq, of, om_out, od_out,
    qm, gm, om, dm, cosr, sinr, turned,
    sbq, sbo, sbf, srvq, srvo, srvf,
    xg, xm, gq, go, gf, acc, scl, near, far, qs, ks, mixed, hidden,
    part, pairs, relay, final, resid, outb, swapb,
    send_sem, sem_a2a, sem_own, sem_w, sem_x, sem_core, sem_rel, sem_fin, sem_swap, loc_sem,
):
    row = lax.axis_index("row")
    col = lax.axis_index("col")
    x = lax.div(row, 4)
    u = lax.rem(lax.div(row, 2), 2)
    c = lax.rem(row, 2)
    h = lax.div(col, 4)
    z = lax.rem(col, 4)
    xp, xn, xo = lax.rem(x + 1, 4), lax.rem(x + 3, 4), lax.rem(x + 2, 4)
    zp, zn, zo = lax.rem(z + 1, 4), lax.rem(z + 3, 4), lax.rem(z + 2, 4)
    source = c == h
    mine = c * 4 + z
    yy = h * 2 + u
    yp, yn, yo = lax.rem(yy + 1, 4), lax.rem(yy + 3, 4), lax.rem(yy + 2, 4)

    def device(xx, uu, cc, hh, zz):
        return (xx * 4 + uu * 2 + cc, hh * 4 + zz)

    to_core = device(x, u, 1 - c, h, z)
    to_swap = device(x, u, h, c, z)
    to_xp, to_xn = device(xp, u, c, h, z), device(xn, u, c, h, z)
    to_zp, to_zn = device(x, u, c, h, zp), device(x, u, c, h, zn)
    to_yp = device(x, lax.rem(yp, 2), c, lax.div(yp, 2), z)
    to_yn = device(x, lax.rem(yn, 2), c, lax.div(yn, 2), z)

    def post(src, dst, sent, recv, target):
        pltpu.make_async_remote_copy(
            src_ref=src,
            dst_ref=dst,
            send_sem=send_sem.at[sent],
            recv_sem=recv,
            device_id=target,
            device_id_type=MESH,
        ).start()

    def arrived(ref, recv):
        pltpu.make_async_remote_copy(
            src_ref=ref,
            dst_ref=ref,
            send_sem=send_sem.at[0],
            recv_sem=recv,
            device_id=to_core,
            device_id_type=MESH,
        ).wait_recv()

    def gone(ref, sent):
        pltpu.make_async_remote_copy(
            src_ref=ref,
            dst_ref=ref,
            send_sem=send_sem.at[sent],
            recv_sem=sem_swap.at[0],
            device_id=to_core,
            device_id_type=MESH,
        ).wait_send()

    loads = [
        pltpu.make_async_copy(src, dst, loc_sem.at[i])
        for i, (src, dst) in enumerate(
            ((qm_hbm, qm), (om_hbm, om), (gm_hbm, gm), (dm_hbm, dm), (cos_hbm, cosr), (sin_hbm, sinr))
        )
    ]
    for one in loads:
        one.start()

    barrier = pltpu.get_barrier_semaphore()
    others = [lax.rem(mine + i, 8) for i in range(1, 8)]
    peers = [device(x, u, lax.div(other, 4), h, lax.rem(other, 4)) for other in others]
    swap_peer = device(x, u, 1 - c, 1 - h, z)
    greet = peers + [swap_peer, to_xp, to_xn, to_yp, to_yn]
    for peer in greet:
        pl.semaphore_signal(barrier, inc=1, device_id=peer, device_id_type=MESH)
    loads[0].wait()
    for i in range(8):
        sbq[i] = qm[:, i * WIDE : (i + 1) * WIDE].astype(BF)
    pl.semaphore_wait(barrier, len(greet))

    def dealt(buf, cc, zz, lo, width):
        start = (x * 4 + u * 2 + cc) * 128 + h * 64 + zz * 16
        return buf.at[pl.ds(pl.multiple_of(start, 16), 16), pl.ds(lo, width)]

    def exchange(send, buf, group, lo, width):
        for i in range(1, 8):
            other = lax.rem(mine + i, 8)
            post(
                send.at[other],
                dealt(buf, c, z, lo, width),
                group,
                sem_a2a.at[group],
                device(x, u, lax.div(other, 4), h, lax.rem(other, 4)),
            )
        start = (x * 4 + u * 2 + c) * 128 + h * 64 + z * 16
        buf[pl.ds(pl.multiple_of(start, 16), 16), lo : lo + width] = send[mine]

    def exchanged(buf, group, lo, width):
        arrived(buf.at[0:112, lo : lo + width], sem_a2a.at[group])

    exchange(sbq, gq, 0, 0, WIDE)

    def lanes(slot):
        return pl.ds(pl.multiple_of(slot * FEAT, FEAT), FEAT)

    def start_swap():
        @pl.when(jnp.logical_not(source))
        def _():
            post(hid, xg.at[:, lanes(col)], 3, sem_swap.at[0], to_swap)

        @pl.when(source)
        def _():
            pltpu.make_async_copy(hid, xg.at[:, lanes(col)], loc_sem.at[6]).start()

    def end_swap():
        @pl.when(jnp.logical_not(source))
        def _():
            arrived(xg.at[:, lanes(mine)], sem_swap.at[0])

        @pl.when(source)
        def _():
            pltpu.make_async_copy(hid, xg.at[:, lanes(col)], loc_sem.at[6]).wait()

    start_swap()

    for one in loads[1:]:
        one.wait()
    for i in range(8):
        sbo[i] = om[:, i * VAL : (i + 1) * VAL].astype(BF)
        sbf[i, :, 0:512] = gm[0, :, i * 512 : (i + 1) * 512].astype(BF)
        sbf[i, :, 512:1024] = gm[1, :, i * 512 : (i + 1) * 512].astype(BF)
        sbf[i, :, 1024:1536] = dm[:, i * 512 : (i + 1) * 512].astype(BF)
    exchange(sbo, go, 1, 0, 512)
    exchange(sbf, gf, 2, 0, 1536)

    head = c * 4 + z
    rate = jnp.float32(0.0)
    for i in range(HEADS):
        rate = jnp.where(head == i, jnp.float32(math.log1p(-(2.0 ** (-5 - i)))), rate)
    lag = lax.broadcasted_iota(jnp.int32, (BLOCK, BLOCK), 0) - lax.broadcasted_iota(
        jnp.int32, (BLOCK, BLOCK), 1
    )
    near[...] = jnp.where(lag >= 0, jnp.exp(jnp.maximum(lag, 0).astype(F32) * rate), 0.0)
    far[...] = jnp.exp((lag + BLOCK).astype(F32) * rate)

    def act_ref(buf, rows, slot):
        return buf.at[rows, lanes(slot)]

    def gather_post(buf, rows, slot, bank, kind, to):
        ref = act_ref(buf, rows, slot)
        post(ref, ref, 4 + bank, sem_x.at[bank * 4 + kind], to)

    def gather_start(buf, first, size, bank):
        rows = pl.ds(first, size)
        gather_post(buf, rows, mine, bank, 0, to_zp)
        gather_post(buf, rows, mine, bank, 1, to_zn)
        gather_post(buf, rows, mine, bank, 3, to_core)

    def gather_near(buf, first, size, bank):
        rows = pl.ds(first, size)
        half = size // 2
        for kind, zz, start, to in ((0, zn, first, to_zp), (1, zp, first + half, to_zn)):
            slot = c * 4 + zz
            arrived(act_ref(buf, rows, slot), sem_x.at[bank * 4 + kind])
            gather_post(buf, pl.ds(start, half), slot, bank, 2, to)
            gather_post(buf, rows, slot, bank, 3, to_core)

    def gather_far(buf, first, size, bank):
        rows = pl.ds(first, size)
        slot = c * 4 + zo
        arrived(act_ref(buf, rows, slot), sem_x.at[bank * 4 + 2])
        gather_post(buf, rows, slot, bank, 3, to_core)

    def gather_core(buf, first, size, bank):
        theirs = pl.ds(pl.multiple_of((1 - c) * 1024, 1024), 1024)
        arrived(buf.at[pl.ds(first, size), theirs], sem_x.at[bank * 4 + 3])

    def gather_gone(buf, first, size, bank):
        gone(buf.at[pl.ds(first, size), 0 : 7 * FEAT], 4 + bank)

    def weights(buf, bank, lo, width):
        xs, ys = (x, xn, xp, xo), (yy, yn, yp, yo)
        cut = pl.ds(lo, width)

        def block(key, half=None):
            xx, where, cc = key
            start = (xx * 4 + lax.rem(where, 2) * 2 + cc) * 128 + lax.div(where, 2) * 64
            if half is None:
                return buf.at[pl.ds(pl.multiple_of(start, 64), 64), cut]
            return buf.at[pl.ds(pl.multiple_of(start + half * 32, 32), 32), cut]

        def send(key, to, kind, half=None):
            ref = block(key, half)
            post(ref, ref, 7 + bank, sem_w.at[bank * 19 + kind], to)

        def wait(key, kind):
            arrived(block(key), sem_w.at[bank * 19 + kind])

        def start():
            for to, kind in ((to_xp, 0), (to_xn, 2), (to_yp, 6), (to_yn, 6)):
                send((x, yy, 0), to, kind)
            for to, kind in ((to_yp, 1), (to_yn, 3), (to_xp, 10), (to_xn, 10)):
                send((x, yy, 1), to, kind)

        def early(i):
            key = (
                (xn, yy, 0), (x, yn, 1), (xp, yy, 0), (x, yp, 1), (xo, yy, 0), (x, yo, 1)
            )[i]
            wait(key, i)
            if i < 4:
                send(key, (to_xp, to_yp, to_xn, to_yn)[i], 4 + i % 2, i // 2)
            place = i // 2 + 1
            if i % 2 == 0:
                send(key, to_yp, 6 + place)
                send(key, to_yn, 6 + place)
            else:
                send(key, to_xp, 10 + place)
                send(key, to_xn, 10 + place)

        def late(i):
            arrived(buf.at[0:128, cut], sem_w.at[bank * 19 + 6 + i])
            if i in (0, 3):
                send((xs[i], yn, 0), to_yp, 14 + i)
            else:
                send((xs[i], yp, 0), to_yn, 14 + i)
            arrived(buf.at[0:128, cut], sem_w.at[bank * 19 + 10 + i])
            if i in (0, 3):
                send((xn, ys[i], 1), to_xp, 18)
            else:
                send((xp, ys[i], 1), to_xn, 18)

        def last(i):
            wait((xs[i], yo, 0), 14 + i)
            if i == 3:
                arrived(buf.at[0:256, cut], sem_w.at[bank * 19 + 18])

        def left():
            gone(buf.at[0:1920, cut], 7 + bank)

        return start, early, late, last, left

    start_q, early_q, late_q, last_q, left_q = weights(gq, 0, 0, WIDE)
    start_o, early_o, late_o, last_o, left_o = weights(go, 1, 0, 512)
    start_g, early_g, late_g, last_g, left_g = weights(gf, 2, 0, 1024)
    start_d, early_d, late_d, last_d, left_d = weights(gf, 3, 1024, 512)

    def serve_start():
        theirs = pl.ds(pl.multiple_of((x * 4 + u * 2 + 1 - c) * 128, 128), 128)
        ours = pl.ds(pl.multiple_of(row * 128, 128), 128)

        @pl.when(source)
        def _():
            for i, (buf, srv) in enumerate(((gq, srvq), (go, srvo), (gf, srvf))):
                post(buf.at[theirs, :], srv, 11 + i, sem_own.at[i], to_core)
                srv[...] = buf[ours, :]

    def serve_end():
        @pl.when(jnp.logical_not(source))
        def _():
            for i, srv in enumerate((srvq, srvo, srvf)):
                arrived(srv, sem_own.at[i])

        store_weights()

    def stores():
        return [
            pltpu.make_async_copy(srvq, oq, loc_sem.at[7]),
            pltpu.make_async_copy(srvf.at[:, 0:512], of.at[0], loc_sem.at[8]),
            pltpu.make_async_copy(srvf.at[:, 512:1024], of.at[1], loc_sem.at[9]),
            pltpu.make_async_copy(turned.at[0], om_out, loc_sem.at[10]),
            pltpu.make_async_copy(turned.at[1], od_out, loc_sem.at[11]),
        ]

    def store_weights():
        turned[0] = jnp.transpose(srvo[...])
        turned[1] = jnp.transpose(srvf[:, 1024:1536])
        for one in stores():
            one.start()

    def scales(buf, first):
        @pl.loop(0, S // 128)
        def _(i):
            rows = pl.ds(pl.multiple_of(first + i * 128, 128), 128)
            tokens = buf[rows, :].astype(F32)
            total = jnp.sum(tokens * tokens, axis=1, keepdims=True)
            scl[rows, :] = jnp.broadcast_to(lax.rsqrt(total * (1.0 / D) + EPS), (128, 128))

    def project(i):
        feats = pl.ds(pl.multiple_of((x, xn, xp, xo)[i] * 512, 512), 512)

        @pl.loop(0, WIDE // 256)
        def _(n):
            wide = pl.ds(pl.multiple_of(n * 256, 256), 256)
            for m in range(REQS):
                rows = pl.ds(m * S, S)
                term = jnp.dot(xg[rows, feats], gq[feats, wide], preferred_element_type=F32)
                if i == 0:
                    acc[rows, wide] = term
                else:
                    acc[rows, wide] += term

    def retention(r):
        first = r * S
        rows = pl.ds(first, S)
        scale = scl[rows, :]
        for ref, at, gain in ((qs, 0, 1.0), (ks, KEY, 1.0 / math.sqrt(KEY))):
            a = (acc[rows, at : at + 128] * scale).astype(BF).astype(F32)
            b = (acc[rows, at + 128 : at + 256] * scale).astype(BF).astype(F32)
            ref[:, 0:128] = ((a * cosr[...] - b * sinr[...]) * gain).astype(BF)
            ref[:, 128:256] = ((a * sinr[...] + b * cosr[...]) * gain).astype(BF)
        wide_scale = jnp.concatenate([scale] * 4, axis=1)
        value = (acc[rows, 512:1024] * wide_scale).astype(BF)
        for t in range(S // BLOCK):
            q = qs[t * BLOCK : (t + 1) * BLOCK, :]
            total = jnp.zeros((BLOCK, VAL), F32)
            denom = jnp.zeros((BLOCK, 1), F32)
            for s in range(t + 1):
                k = ks[s * BLOCK : (s + 1) * BLOCK, :]
                score = lax.dot_general(q, k, NT, preferred_element_type=F32)
                score = score * (near[...] if s == t else far[...])
                denom += jnp.sum(score, axis=1, keepdims=True)
                total += jnp.dot(
                    score.astype(BF),
                    value[s * BLOCK : (s + 1) * BLOCK, :],
                    preferred_element_type=F32,
                )
            kept = total / jnp.maximum(jnp.abs(denom), 1.0)
            centred = kept - jnp.mean(kept, axis=1, keepdims=True)
            spread = jnp.mean(centred * centred, axis=1, keepdims=True)
            block = pl.ds(first + t * BLOCK, BLOCK)
            gate = (acc[block, 1024:1536] * wide_scale[t * BLOCK : (t + 1) * BLOCK, :]).astype(BF)
            mixed[block, :] = (
                jax.nn.silu(gate.astype(F32)) * (centred * lax.rsqrt(spread + EPS))
            ).astype(BF)

    def terms(left, weight, at, r, bank):
        rows = pl.ds(r * S, S)

        def term(slot):
            feats = pl.ds(pl.multiple_of(slot * FEAT, FEAT), FEAT)
            part[r, slot] = lax.dot_general(
                left[rows, :], weight[feats, at : at + 512], NT, preferred_element_type=F32
            ).astype(BF)

        @pl.loop(0, 4)
        def _(j):
            zz = lax.rem(zo + j, 4)
            slot = (1 - c) * 4 + zz
            term(slot)
            post(
                part.at[r, slot],
                pairs.at[bank, r, zz],
                14 + bank * 2 + r,
                sem_core.at[bank * 8 + r * 4 + zz],
                to_core,
            )

        @pl.loop(0, 4)
        def _(j):
            term(c * 4 + lax.rem(zo + j, 4))

    HALF = S // 2
    TOP, BOT = pl.ds(0, HALF), pl.ds(HALF, HALF)

    def pair(r, bank, zz):
        arrived(pairs.at[bank, r, zz], sem_core.at[bank * 8 + r * 4 + zz])
        slot = c * 4 + zz
        return slot

    def both(r, bank, zz, rows):
        return part[r, c * 4 + zz, rows, :].astype(F32) + pairs[bank, r, zz, rows, :].astype(F32)

    def reduce_start(r, bank):
        rel = (bank * 2 + r) * 2
        slot = pair(r, bank, zo)
        part[r, slot] = both(r, bank, zo, pl.ds(0, S)).astype(BF)
        post(part.at[r, slot, TOP, :], relay.at[bank, r, 0], 18 + bank * 2 + r, sem_rel.at[rel], to_zp)
        post(part.at[r, slot, BOT, :], relay.at[bank, r, 1], 18 + bank * 2 + r, sem_rel.at[rel + 1], to_zn)
        slot = pair(r, bank, zp)
        part[r, slot, BOT, :] = both(r, bank, zp, BOT).astype(BF)
        post(part.at[r, slot, BOT, :], final.at[bank, r, 0, BOT, :], 18 + bank * 2 + r, sem_fin.at[bank * 2 + r], to_zp)
        slot = pair(r, bank, zn)
        part[r, slot, TOP, :] = both(r, bank, zn, TOP).astype(BF)
        post(part.at[r, slot, TOP, :], final.at[bank, r, 1, TOP, :], 18 + bank * 2 + r, sem_fin.at[bank * 2 + r], to_zn)

    def reduce_relay(r, bank):
        rel = (bank * 2 + r) * 2
        arrived(relay.at[bank, r, 0], sem_rel.at[rel])
        slot = c * 4 + zp
        part[r, slot, TOP, :] = (both(r, bank, zp, TOP) + relay[bank, r, 0].astype(F32)).astype(BF)
        post(part.at[r, slot, TOP, :], final.at[bank, r, 0, TOP, :], 18 + bank * 2 + r, sem_fin.at[bank * 2 + r], to_zp)
        arrived(relay.at[bank, r, 1], sem_rel.at[rel + 1])
        slot = c * 4 + zn
        part[r, slot, BOT, :] = (both(r, bank, zn, BOT) + relay[bank, r, 1].astype(F32)).astype(BF)
        post(part.at[r, slot, BOT, :], final.at[bank, r, 1, BOT, :], 18 + bank * 2 + r, sem_fin.at[bank * 2 + r], to_zn)
        pair(r, bank, z)

    def reduce_end(r, bank):
        arrived(final.at[bank, r], sem_fin.at[bank * 2 + r])
        return (
            both(r, bank, z, pl.ds(0, S))
            + final[bank, r, 0].astype(F32)
            + final[bank, r, 1].astype(F32)
        )

    def reduce_gone(r, bank):
        gone(part.at[r, 0:4], 14 + bank * 2 + r)
        gone(part.at[r, 0:3], 18 + bank * 2 + r)

    def add_residual(r):
        rows = pl.ds(r * S, S)
        total = xg[rows, lanes(mine)].astype(F32) + reduce_end(r, 0)
        resid[rows, :] = total
        xm[rows, lanes(mine)] = total.astype(BF)

    def feed(r):
        rows = pl.ds(r * S, S)
        scales(xm, r * S)
        scale = jnp.concatenate([scl[rows, :]] * 2, axis=1)

        @pl.loop(0, 2)
        def _(n):
            at = pl.ds(pl.multiple_of(n * 256, 256), 256)
            up_at = pl.ds(pl.multiple_of(512 + n * 256, 256), 256)
            gate = jnp.dot(xm[rows, :], gf[:, at], preferred_element_type=F32) * scale
            up = jnp.dot(xm[rows, :], gf[:, up_at], preferred_element_type=F32) * scale
            hidden[rows, at] = (jax.nn.silu(gate) * up).astype(BF)

    def finish(r):
        rows = pl.ds(r * S, S)
        outb[rows, :] = (resid[rows, :] + reduce_end(r, 1)).astype(BF)

        @pl.when(jnp.logical_not(source))
        def _():
            post(outb.at[rows, :], swapb.at[rows, :], 22 + r, sem_swap.at[1 + r], to_swap)

    def save(r):
        rows = pl.ds(r * S, S)
        live = lax.broadcasted_iota(jnp.int32, (S, FEAT), 0) < lens[r]

        @pl.when(source)
        def _():
            swapb[rows, :] = jnp.where(live, outb[rows, :], jnp.zeros((S, FEAT), BF))

        @pl.when(jnp.logical_not(source))
        def _():
            arrived(swapb.at[rows, :], sem_swap.at[1 + r])
            swapb[rows, :] = jnp.where(live, swapb[rows, :], jnp.zeros((S, FEAT), BF))

        pltpu.make_async_copy(swapb.at[rows, :], y.at[rows, :], loc_sem.at[12 + r]).start()

    def saved(r):
        rows = pl.ds(r * S, S)
        pltpu.make_async_copy(swapb.at[rows, :], y.at[rows, :], loc_sem.at[12 + r]).wait()

    def out(r):
        terms(mixed, go, 0, r, 0)

    def down(r):
        reduce_gone(r, 0)
        terms(hidden, gf, 1024, r, 1)

    def act(step, r):
        step(xm, r * S, S, 1 + r)

    exchanged(gq, 0, 0, WIDE)
    start_q()
    end_swap()
    gather_start(xg, 0, TOK, 0)
    exchanged(go, 1, 0, 512)
    exchanged(gf, 2, 0, 1536)
    early_q(0)
    early_q(1)
    early_q(2)
    early_q(3)
    gather_near(xg, 0, TOK, 0)
    early_q(4)
    early_q(5)
    gather_far(xg, 0, TOK, 0)
    late_q(0)
    gather_core(xg, 0, TOK, 0)
    scales(xg, 0)
    late_q(1)
    scales(xg, S)
    start_o()
    late_q(2)
    last_q(0)
    project(0)
    late_q(3)
    last_q(1)
    project(1)
    last_q(2)
    project(2)
    early_o(0)
    early_o(1)
    early_o(2)
    early_o(3)
    start_g()
    last_q(3)
    project(3)
    early_o(4)
    early_o(5)
    late_o(0)
    retention(0)
    late_o(1)
    late_o(2)
    late_o(3)
    early_g(0)
    early_g(1)
    early_g(2)
    early_g(3)
    start_d()
    retention(1)
    last_o(0)
    last_o(1)
    last_o(2)
    last_o(3)
    early_g(4)
    early_g(5)
    out(0)
    late_g(0)
    late_g(1)
    out(1)
    late_g(2)
    reduce_start(0, 0)
    late_g(3)
    reduce_start(1, 0)
    reduce_relay(0, 0)
    early_d(0)
    early_d(1)
    early_d(2)
    early_d(3)
    reduce_relay(1, 0)
    early_d(4)
    early_d(5)
    add_residual(0)
    act(gather_start, 0)
    late_d(0)
    add_residual(1)
    act(gather_start, 1)
    late_d(1)
    late_d(2)
    act(gather_near, 0)
    late_d(3)
    act(gather_far, 0)
    act(gather_near, 1)
    act(gather_core, 0)
    last_g(0)
    last_g(1)
    last_g(2)
    last_g(3)
    feed(0)
    act(gather_far, 1)
    last_d(0)
    last_d(1)
    last_d(2)
    last_d(3)
    down(0)
    act(gather_core, 1)
    serve_start()
    reduce_start(0, 1)
    feed(1)
    reduce_relay(0, 1)
    down(1)
    serve_end()
    reduce_start(1, 1)
    finish(0)
    reduce_relay(1, 1)
    save(0)
    finish(1)
    save(1)

    for group, (buf, lo, width) in enumerate(((gq, 0, WIDE), (go, 0, 512), (gf, 0, 1536))):
        gone(buf.at[0:112, lo : lo + width], group)
    gather_gone(xg, 0, TOK, 0)
    for r in range(REQS):
        act(gather_gone, r)
        reduce_gone(r, 1)
    left_q()
    left_o()
    left_g()
    left_d()

    @pl.when(source)
    def _():
        for i, srv in enumerate((srvq, srvo, srvf)):
            gone(srv, 11 + i)

    @pl.when(jnp.logical_not(source))
    def _():
        gone(hid, 3)
        for r in range(REQS):
            gone(outb.at[pl.ds(r * S, S), :], 22 + r)

    for one in stores():
        one.wait()
    saved(0)
    saved(1)


def settle(y_in, q_in, f_in, m_in, d_in, y, q, f, m, d, yv, qv, fv, mv, dv, sem):
    sets = ((y_in, yv, y), (q_in, qv, q), (f_in, fv, f), (m_in, mv, m), (d_in, dv, d))
    takes = [pltpu.make_async_copy(a, b, sem.at[i]) for i, (a, b, _) in enumerate(sets)]
    gives = [pltpu.make_async_copy(b, c, sem.at[5 + i]) for i, (_, b, c) in enumerate(sets)]
    for one in takes:
        one.start()
    for one, two in zip(takes, gives):
        one.wait()
        two.start()
    for one in gives:
        one.wait()


def layer(lengths, hidden, qkvg, gateup, out_t, down_t):
    cosine, sine = tables()
    hbm = pl.BlockSpec(memory_space=pl.ANY)
    dma = pltpu.SemaphoreType.DMA
    shapes = (
        jax.ShapeDtypeStruct((TOK, FEAT), BF),
        jax.ShapeDtypeStruct((128, WIDE), BF),
        jax.ShapeDtypeStruct((2, 128, 512), BF),
        jax.ShapeDtypeStruct((512, 128), BF),
        jax.ShapeDtypeStruct((512, 128), BF),
    )
    scratch = [
        pltpu.VMEM((16, HEADS * WIDE), F32),
        pltpu.VMEM((2, 16, FF), F32),
        pltpu.VMEM((16, HEADS * VAL), F32),
        pltpu.VMEM((16, FF), F32),
        pltpu.VMEM((S, KEY // 2), F32),
        pltpu.VMEM((S, KEY // 2), F32),
        pltpu.VMEM((2, 512, 128), BF),
        pltpu.VMEM((8, 16, WIDE), BF),
        pltpu.VMEM((8, 16, 512), BF),
        pltpu.VMEM((8, 16, 1536), BF),
        pltpu.VMEM((128, WIDE), BF),
        pltpu.VMEM((128, 512), BF),
        pltpu.VMEM((128, 1536), BF),
        pltpu.VMEM((TOK, D), BF),
        pltpu.VMEM((TOK, D), BF),
        pltpu.VMEM((D, WIDE), BF),
        pltpu.VMEM((D, 512), BF),
        pltpu.VMEM((D, 1536), BF),
        pltpu.VMEM((TOK, WIDE), F32),
        pltpu.VMEM((TOK, 128), F32),
        pltpu.VMEM((BLOCK, BLOCK), F32),
        pltpu.VMEM((BLOCK, BLOCK), F32),
        pltpu.VMEM((S, KEY), BF),
        pltpu.VMEM((S, KEY), BF),
        pltpu.VMEM((TOK, VAL), BF),
        pltpu.VMEM((TOK, 512), BF),
        pltpu.VMEM((REQS, 8, S, FEAT), BF),
        pltpu.VMEM((2, REQS, 4, S, FEAT), BF),
        pltpu.VMEM((2, REQS, 2, S // 2, FEAT), BF),
        pltpu.VMEM((2, REQS, 2, S, FEAT), BF),
        pltpu.VMEM((TOK, FEAT), F32),
        pltpu.VMEM((TOK, FEAT), BF),
        pltpu.VMEM((TOK, FEAT), BF),
        dma((24,)),
        dma((3,)),
        dma((3,)),
        dma((76,)),
        dma((12,)),
        dma((16,)),
        dma((8,)),
        dma((4,)),
        dma((3,)),
        dma((14,)),
    ]
    results = pl.pallas_call(
        kernel,
        out_shape=shapes,
        in_specs=[pl.BlockSpec(memory_space=pltpu.SMEM)] + [hbm] * 7,
        out_specs=(hbm,) * 5,
        scratch_shapes=scratch,
        compiler_params=pltpu.CompilerParams(
            collective_id=0, has_side_effects=True, vmem_limit_bytes=62 * 1024 * 1024
        ),
    )(lengths, hidden, qkvg, gateup, out_t, down_t, jnp.asarray(cosine), jnp.asarray(sine))
    return pl.pallas_call(
        settle,
        out_shape=shapes,
        in_specs=[hbm] * 5,
        out_specs=(hbm,) * 5,
        scratch_shapes=[pltpu.VMEM(one.shape, one.dtype) for one in shapes] + [dma((10,))],
    )(*results)


def shards(hidden_states, lengths, qkvg_master, gateup_master, out_master, down_master):
    return layer(
        lengths, hidden_states, qkvg_master, gateup_master, out_master.T, down_master.T
    )


def solution(mesh):
    return jax.shard_map(
        shards,
        mesh=mesh,
        in_specs=(
            P("row", "col"),
            P("row"),
            P(("row", "col"), None),
            P(None, ("row", "col"), None),
            P(None, ("row", "col")),
            P(None, ("row", "col")),
        ),
        out_specs=(
            P("row", "col"),
            P("row", "col"),
            P(None, "row", "col"),
            P("col", "row"),
            P("col", "row"),
        ),
        check_vma=False,
    )
```

```python
import math

import jax
import jax.numpy as jnp
import numpy as np
from jax import lax
from jax.experimental import pallas as pl
from jax.experimental.pallas import tpu as pltpu
from jax.sharding import PartitionSpec as P

D = 2048
HEADS = 8
KEY = 256
VAL = 512
S = 512
BLOCK = 256
FF = 4096
WIDE = 2 * KEY + 2 * VAL
TOK = 1024
FEAT = 256
REQS = 2
EPS = 1e-05
MESH = pl.DeviceIdType.MESH
BF = jnp.bfloat16
F32 = jnp.float32
NT = (((1,), (1,)), ((), ()))


def tables():
    half = KEY // 2
    freq = np.power(np.float32(10000.0), (-2.0 * np.arange(half) / KEY).astype(np.float32))
    angle = np.arange(S, dtype=np.float32)[:, None] * freq.astype(np.float32)[None, :]
    return np.cos(angle).astype(np.float32), np.sin(angle).astype(np.float32)


def kernel(
    lens, hid, qm_hbm, gm_hbm, om_hbm, dm_hbm, cos_hbm, sin_hbm,
    y, oq, of, om_out, od_out,
    qm, gm, om, dm, cosr, sinr, turned,
    sbq, sbo, sbf, srvq, srvo, srvf,
    xg, xm, gq, go, gf, acc, scl, near, far, qs, ks, mixed, hidden,
    part, pairs, relay, final, resid, outb, swapb,
    send_sem, sem_a2a, sem_own, sem_w, sem_x, sem_core, sem_rel, sem_fin, sem_swap, loc_sem,
):
    row = lax.axis_index("row")
    col = lax.axis_index("col")
    x = lax.div(row, 4)
    u = lax.rem(lax.div(row, 2), 2)
    c = lax.rem(row, 2)
    h = lax.div(col, 4)
    z = lax.rem(col, 4)
    xp, xn, xo = lax.rem(x + 1, 4), lax.rem(x + 3, 4), lax.rem(x + 2, 4)
    zp, zn, zo = lax.rem(z + 1, 4), lax.rem(z + 3, 4), lax.rem(z + 2, 4)
    source = c == h
    mine = c * 4 + z
    yy = h * 2 + u
    yp, yn, yo = lax.rem(yy + 1, 4), lax.rem(yy + 3, 4), lax.rem(yy + 2, 4)

    def device(xx, uu, cc, hh, zz):
        return (xx * 4 + uu * 2 + cc, hh * 4 + zz)

    to_core = device(x, u, 1 - c, h, z)
    to_swap = device(x, u, h, c, z)
    to_xp, to_xn = device(xp, u, c, h, z), device(xn, u, c, h, z)
    to_zp, to_zn = device(x, u, c, h, zp), device(x, u, c, h, zn)
    to_yp = device(x, lax.rem(yp, 2), c, lax.div(yp, 2), z)
    to_yn = device(x, lax.rem(yn, 2), c, lax.div(yn, 2), z)

    def post(src, dst, sent, recv, target):
        pltpu.make_async_remote_copy(
            src_ref=src,
            dst_ref=dst,
            send_sem=send_sem.at[sent],
            recv_sem=recv,
            device_id=target,
            device_id_type=MESH,
        ).start()

    def arrived(ref, recv):
        pltpu.make_async_remote_copy(
            src_ref=ref,
            dst_ref=ref,
            send_sem=send_sem.at[0],
            recv_sem=recv,
            device_id=to_core,
            device_id_type=MESH,
        ).wait_recv()

    def gone(ref, sent):
        pltpu.make_async_remote_copy(
            src_ref=ref,
            dst_ref=ref,
            send_sem=send_sem.at[sent],
            recv_sem=sem_swap.at[0],
            device_id=to_core,
            device_id_type=MESH,
        ).wait_send()

    loads = [
        pltpu.make_async_copy(src, dst, loc_sem.at[i])
        for i, (src, dst) in enumerate(
            ((qm_hbm, qm), (om_hbm, om), (gm_hbm, gm), (dm_hbm, dm), (cos_hbm, cosr), (sin_hbm, sinr))
        )
    ]
    for one in loads:
        one.start()

    barrier = pltpu.get_barrier_semaphore()
    others = [lax.rem(mine + i, 8) for i in range(1, 8)]
    peers = [device(x, u, lax.div(other, 4), h, lax.rem(other, 4)) for other in others]
    swap_peer = device(x, u, 1 - c, 1 - h, z)
    greet = peers + [swap_peer, to_xp, to_xn, to_yp, to_yn]
    for peer in greet:
        pl.semaphore_signal(barrier, inc=1, device_id=peer, device_id_type=MESH)
    loads[0].wait()
    for i in range(8):
        sbq[i] = qm[:, i * WIDE : (i + 1) * WIDE].astype(BF)
    pl.semaphore_wait(barrier, len(greet))

    def dealt(buf, cc, zz, lo, width):
        start = (x * 4 + u * 2 + cc) * 128 + h * 64 + zz * 16
        return buf.at[pl.ds(pl.multiple_of(start, 16), 16), pl.ds(lo, width)]

    def exchange(send, buf, group, lo, width):
        for i in range(1, 8):
            other = lax.rem(mine + i, 8)
            post(
                send.at[other],
                dealt(buf, c, z, lo, width),
                group,
                sem_a2a.at[group],
                device(x, u, lax.div(other, 4), h, lax.rem(other, 4)),
            )
        start = (x * 4 + u * 2 + c) * 128 + h * 64 + z * 16
        buf[pl.ds(pl.multiple_of(start, 16), 16), lo : lo + width] = send[mine]

    def exchanged(buf, group, lo, width):
        arrived(buf.at[0:112, lo : lo + width], sem_a2a.at[group])

    exchange(sbq, gq, 0, 0, WIDE)

    def lanes(slot):
        return pl.ds(pl.multiple_of(slot * FEAT, FEAT), FEAT)

    def start_swap():
        @pl.when(jnp.logical_not(source))
        def _():
            post(hid, xg.at[:, lanes(col)], 3, sem_swap.at[0], to_swap)

        @pl.when(source)
        def _():
            pltpu.make_async_copy(hid, xg.at[:, lanes(col)], loc_sem.at[6]).start()

    def end_swap():
        @pl.when(jnp.logical_not(source))
        def _():
            arrived(xg.at[:, lanes(mine)], sem_swap.at[0])

        @pl.when(source)
        def _():
            pltpu.make_async_copy(hid, xg.at[:, lanes(col)], loc_sem.at[6]).wait()

    start_swap()

    for one in loads[1:]:
        one.wait()
    for i in range(8):
        sbo[i] = om[:, i * VAL : (i + 1) * VAL].astype(BF)
        sbf[i, :, 0:512] = gm[0, :, i * 512 : (i + 1) * 512].astype(BF)
        sbf[i, :, 512:1024] = gm[1, :, i * 512 : (i + 1) * 512].astype(BF)
        sbf[i, :, 1024:1536] = dm[:, i * 512 : (i + 1) * 512].astype(BF)
    exchange(sbo, go, 1, 0, 512)
    exchange(sbf, gf, 2, 0, 1536)

    head = c * 4 + z
    rate = jnp.float32(0.0)
    for i in range(HEADS):
        rate = jnp.where(head == i, jnp.float32(math.log1p(-(2.0 ** (-5 - i)))), rate)
    lag = lax.broadcasted_iota(jnp.int32, (BLOCK, BLOCK), 0) - lax.broadcasted_iota(
        jnp.int32, (BLOCK, BLOCK), 1
    )
    near[...] = jnp.where(lag >= 0, jnp.exp(jnp.maximum(lag, 0).astype(F32) * rate), 0.0)
    far[...] = jnp.exp((lag + BLOCK).astype(F32) * rate)

    def act_ref(buf, rows, slot):
        return buf.at[rows, lanes(slot)]

    def gather_post(buf, rows, slot, bank, kind, to):
        ref = act_ref(buf, rows, slot)
        post(ref, ref, 4 + bank, sem_x.at[bank * 4 + kind], to)

    def gather_start(buf, first, size, bank):
        rows = pl.ds(first, size)
        gather_post(buf, rows, mine, bank, 0, to_zp)
        gather_post(buf, rows, mine, bank, 1, to_zn)
        gather_post(buf, rows, mine, bank, 3, to_core)

    def gather_near(buf, first, size, bank):
        rows = pl.ds(first, size)
        half = size // 2
        for kind, zz, start, to in ((0, zn, first, to_zp), (1, zp, first + half, to_zn)):
            slot = c * 4 + zz
            arrived(act_ref(buf, rows, slot), sem_x.at[bank * 4 + kind])
            gather_post(buf, pl.ds(start, half), slot, bank, 2, to)
            gather_post(buf, rows, slot, bank, 3, to_core)

    def gather_far(buf, first, size, bank):
        rows = pl.ds(first, size)
        slot = c * 4 + zo
        arrived(act_ref(buf, rows, slot), sem_x.at[bank * 4 + 2])
        gather_post(buf, rows, slot, bank, 3, to_core)

    def gather_core(buf, first, size, bank):
        theirs = pl.ds(pl.multiple_of((1 - c) * 1024, 1024), 1024)
        arrived(buf.at[pl.ds(first, size), theirs], sem_x.at[bank * 4 + 3])

    def gather_gone(buf, first, size, bank):
        gone(buf.at[pl.ds(first, size), 0 : 7 * FEAT], 4 + bank)

    def weights(buf, bank, lo, width):
        xs, ys = (x, xn, xp, xo), (yy, yn, yp, yo)
        cut = pl.ds(lo, width)

        def block(key, half=None):
            xx, where, cc = key
            start = (xx * 4 + lax.rem(where, 2) * 2 + cc) * 128 + lax.div(where, 2) * 64
            if half is None:
                return buf.at[pl.ds(pl.multiple_of(start, 64), 64), cut]
            return buf.at[pl.ds(pl.multiple_of(start + half * 32, 32), 32), cut]

        def send(key, to, kind, half=None):
            ref = block(key, half)
            post(ref, ref, 7 + bank, sem_w.at[bank * 19 + kind], to)

        def wait(key, kind):
            arrived(block(key), sem_w.at[bank * 19 + kind])

        def start():
            for to, kind in ((to_xp, 0), (to_xn, 2), (to_yp, 6), (to_yn, 6)):
                send((x, yy, 0), to, kind)
            for to, kind in ((to_yp, 1), (to_yn, 3), (to_xp, 10), (to_xn, 10)):
                send((x, yy, 1), to, kind)

        def early(i):
            key = (
                (xn, yy, 0), (x, yn, 1), (xp, yy, 0), (x, yp, 1), (xo, yy, 0), (x, yo, 1)
            )[i]
            wait(key, i)
            if i < 4:
                send(key, (to_xp, to_yp, to_xn, to_yn)[i], 4 + i % 2, i // 2)
            place = i // 2 + 1
            if i % 2 == 0:
                send(key, to_yp, 6 + place)
                send(key, to_yn, 6 + place)
            else:
                send(key, to_xp, 10 + place)
                send(key, to_xn, 10 + place)

        def late(i):
            arrived(buf.at[0:128, cut], sem_w.at[bank * 19 + 6 + i])
            if i in (0, 3):
                send((xs[i], yn, 0), to_yp, 14 + i)
            else:
                send((xs[i], yp, 0), to_yn, 14 + i)
            arrived(buf.at[0:128, cut], sem_w.at[bank * 19 + 10 + i])
            if i in (0, 3):
                send((xn, ys[i], 1), to_xp, 18)
            else:
                send((xp, ys[i], 1), to_xn, 18)

        def last(i):
            wait((xs[i], yo, 0), 14 + i)
            if i == 3:
                arrived(buf.at[0:256, cut], sem_w.at[bank * 19 + 18])

        def left():
            gone(buf.at[0:1920, cut], 7 + bank)

        return start, early, late, last, left

    start_q, early_q, late_q, last_q, left_q = weights(gq, 0, 0, WIDE)
    start_o, early_o, late_o, last_o, left_o = weights(go, 1, 0, 512)
    start_g, early_g, late_g, last_g, left_g = weights(gf, 2, 0, 1024)
    start_d, early_d, late_d, last_d, left_d = weights(gf, 3, 1024, 512)

    def serve_start():
        theirs = pl.ds(pl.multiple_of((x * 4 + u * 2 + 1 - c) * 128, 128), 128)
        ours = pl.ds(pl.multiple_of(row * 128, 128), 128)

        @pl.when(source)
        def _():
            for i, (buf, srv) in enumerate(((gq, srvq), (go, srvo), (gf, srvf))):
                post(buf.at[theirs, :], srv, 11 + i, sem_own.at[i], to_core)
                srv[...] = buf[ours, :]

    def serve_end():
        @pl.when(jnp.logical_not(source))
        def _():
            for i, srv in enumerate((srvq, srvo, srvf)):
                arrived(srv, sem_own.at[i])

        store_weights()

    def stores():
        return [
            pltpu.make_async_copy(srvq, oq, loc_sem.at[7]),
            pltpu.make_async_copy(srvf.at[:, 0:512], of.at[0], loc_sem.at[8]),
            pltpu.make_async_copy(srvf.at[:, 512:1024], of.at[1], loc_sem.at[9]),
            pltpu.make_async_copy(turned.at[0], om_out, loc_sem.at[10]),
            pltpu.make_async_copy(turned.at[1], od_out, loc_sem.at[11]),
        ]

    def store_weights():
        turned[0] = jnp.transpose(srvo[...])
        turned[1] = jnp.transpose(srvf[:, 1024:1536])
        for one in stores():
            one.start()

    def scales(buf, first):
        @pl.loop(0, S // 128)
        def _(i):
            rows = pl.ds(pl.multiple_of(first + i * 128, 128), 128)
            tokens = buf[rows, :].astype(F32)
            total = jnp.sum(tokens * tokens, axis=1, keepdims=True)
            scl[rows, :] = jnp.broadcast_to(lax.rsqrt(total * (1.0 / D) + EPS), (128, 128))

    def project(i):
        feats = pl.ds(pl.multiple_of((x, xn, xp, xo)[i] * 512, 512), 512)

        @pl.loop(0, WIDE // 256)
        def _(n):
            wide = pl.ds(pl.multiple_of(n * 256, 256), 256)
            for m in range(REQS):
                rows = pl.ds(m * S, S)
                term = jnp.dot(xg[rows, feats], gq[feats, wide], preferred_element_type=F32)
                if i == 0:
                    acc[rows, wide] = term
                else:
                    acc[rows, wide] += term

    def retention(r):
        first = r * S
        rows = pl.ds(first, S)
        scale = scl[rows, :]
        for ref, at, gain in ((qs, 0, 1.0), (ks, KEY, 1.0 / math.sqrt(KEY))):
            a = (acc[rows, at : at + 128] * scale).astype(BF).astype(F32)
            b = (acc[rows, at + 128 : at + 256] * scale).astype(BF).astype(F32)
            ref[:, 0:128] = ((a * cosr[...] - b * sinr[...]) * gain).astype(BF)
            ref[:, 128:256] = ((a * sinr[...] + b * cosr[...]) * gain).astype(BF)
        wide_scale = jnp.concatenate([scale] * 4, axis=1)
        value = (acc[rows, 512:1024] * wide_scale).astype(BF)
        for t in range(S // BLOCK):
            q = qs[t * BLOCK : (t + 1) * BLOCK, :]
            total = jnp.zeros((BLOCK, VAL), F32)
            denom = jnp.zeros((BLOCK, 1), F32)
            for s in range(t + 1):
                k = ks[s * BLOCK : (s + 1) * BLOCK, :]
                score = lax.dot_general(q, k, NT, preferred_element_type=F32)
                score = score * (near[...] if s == t else far[...])
                denom += jnp.sum(score, axis=1, keepdims=True)
                total += jnp.dot(
                    score.astype(BF),
                    value[s * BLOCK : (s + 1) * BLOCK, :],
                    preferred_element_type=F32,
                )
            kept = total / jnp.maximum(jnp.abs(denom), 1.0)
            centred = kept - jnp.mean(kept, axis=1, keepdims=True)
            spread = jnp.mean(centred * centred, axis=1, keepdims=True)
            block = pl.ds(first + t * BLOCK, BLOCK)
            gate = (acc[block, 1024:1536] * wide_scale[t * BLOCK : (t + 1) * BLOCK, :]).astype(BF)
            mixed[block, :] = (
                jax.nn.silu(gate.astype(F32)) * (centred * lax.rsqrt(spread + EPS))
            ).astype(BF)

    def terms(left, weight, at, r, bank):
        rows = pl.ds(r * S, S)

        def term(slot):
            feats = pl.ds(pl.multiple_of(slot * FEAT, FEAT), FEAT)
            part[r, slot] = lax.dot_general(
                left[rows, :], weight[feats, at : at + 512], NT, preferred_element_type=F32
            ).astype(BF)

        @pl.loop(0, 4)
        def _(j):
            zz = lax.rem(zo + j, 4)
            slot = (1 - c) * 4 + zz
            term(slot)
            post(
                part.at[r, slot],
                pairs.at[bank, r, zz],
                14 + bank * 2 + r,
                sem_core.at[bank * 8 + r * 4 + zz],
                to_core,
            )

        @pl.loop(0, 4)
        def _(j):
            term(c * 4 + lax.rem(zo + j, 4))

    HALF = S // 2
    TOP, BOT = pl.ds(0, HALF), pl.ds(HALF, HALF)

    def pair(r, bank, zz):
        arrived(pairs.at[bank, r, zz], sem_core.at[bank * 8 + r * 4 + zz])
        slot = c * 4 + zz
        return slot

    def both(r, bank, zz, rows):
        return part[r, c * 4 + zz, rows, :].astype(F32) + pairs[bank, r, zz, rows, :].astype(F32)

    def reduce_start(r, bank):
        rel = (bank * 2 + r) * 2
        slot = pair(r, bank, zo)
        part[r, slot] = both(r, bank, zo, pl.ds(0, S)).astype(BF)
        post(part.at[r, slot, TOP, :], relay.at[bank, r, 0], 18 + bank * 2 + r, sem_rel.at[rel], to_zp)
        post(part.at[r, slot, BOT, :], relay.at[bank, r, 1], 18 + bank * 2 + r, sem_rel.at[rel + 1], to_zn)
        slot = pair(r, bank, zp)
        part[r, slot, BOT, :] = both(r, bank, zp, BOT).astype(BF)
        post(part.at[r, slot, BOT, :], final.at[bank, r, 0, BOT, :], 18 + bank * 2 + r, sem_fin.at[bank * 2 + r], to_zp)
        slot = pair(r, bank, zn)
        part[r, slot, TOP, :] = both(r, bank, zn, TOP).astype(BF)
        post(part.at[r, slot, TOP, :], final.at[bank, r, 1, TOP, :], 18 + bank * 2 + r, sem_fin.at[bank * 2 + r], to_zn)

    def reduce_relay(r, bank):
        rel = (bank * 2 + r) * 2
        arrived(relay.at[bank, r, 0], sem_rel.at[rel])
        slot = c * 4 + zp
        part[r, slot, TOP, :] = (both(r, bank, zp, TOP) + relay[bank, r, 0].astype(F32)).astype(BF)
        post(part.at[r, slot, TOP, :], final.at[bank, r, 0, TOP, :], 18 + bank * 2 + r, sem_fin.at[bank * 2 + r], to_zp)
        arrived(relay.at[bank, r, 1], sem_rel.at[rel + 1])
        slot = c * 4 + zn
        part[r, slot, BOT, :] = (both(r, bank, zn, BOT) + relay[bank, r, 1].astype(F32)).astype(BF)
        post(part.at[r, slot, BOT, :], final.at[bank, r, 1, BOT, :], 18 + bank * 2 + r, sem_fin.at[bank * 2 + r], to_zn)
        pair(r, bank, z)

    def reduce_end(r, bank):
        arrived(final.at[bank, r], sem_fin.at[bank * 2 + r])
        return (
            both(r, bank, z, pl.ds(0, S))
            + final[bank, r, 0].astype(F32)
            + final[bank, r, 1].astype(F32)
        )

    def reduce_gone(r, bank):
        gone(part.at[r, 0:4], 14 + bank * 2 + r)
        gone(part.at[r, 0:3], 18 + bank * 2 + r)

    def add_residual(r):
        rows = pl.ds(r * S, S)
        total = xg[rows, lanes(mine)].astype(F32) + reduce_end(r, 0)
        resid[rows, :] = total
        xm[rows, lanes(mine)] = total.astype(BF)

    def feed(r):
        rows = pl.ds(r * S, S)
        scales(xm, r * S)
        scale = jnp.concatenate([scl[rows, :]] * 2, axis=1)

        @pl.loop(0, 2)
        def _(n):
            at = pl.ds(pl.multiple_of(n * 256, 256), 256)
            up_at = pl.ds(pl.multiple_of(512 + n * 256, 256), 256)
            gate = jnp.dot(xm[rows, :], gf[:, at], preferred_element_type=F32) * scale
            up = jnp.dot(xm[rows, :], gf[:, up_at], preferred_element_type=F32) * scale
            hidden[rows, at] = (jax.nn.silu(gate) * up).astype(BF)

    def finish(r):
        rows = pl.ds(r * S, S)
        outb[rows, :] = (resid[rows, :] + reduce_end(r, 1)).astype(BF)

        @pl.when(jnp.logical_not(source))
        def _():
            post(outb.at[rows, :], swapb.at[rows, :], 22 + r, sem_swap.at[1 + r], to_swap)

    def save(r):
        rows = pl.ds(r * S, S)
        live = lax.broadcasted_iota(jnp.int32, (S, FEAT), 0) < lens[r]

        @pl.when(source)
        def _():
            swapb[rows, :] = jnp.where(live, outb[rows, :], jnp.zeros((S, FEAT), BF))

        @pl.when(jnp.logical_not(source))
        def _():
            arrived(swapb.at[rows, :], sem_swap.at[1 + r])
            swapb[rows, :] = jnp.where(live, swapb[rows, :], jnp.zeros((S, FEAT), BF))

        pltpu.make_async_copy(swapb.at[rows, :], y.at[rows, :], loc_sem.at[12 + r]).start()

    def saved(r):
        rows = pl.ds(r * S, S)
        pltpu.make_async_copy(swapb.at[rows, :], y.at[rows, :], loc_sem.at[12 + r]).wait()

    def out(r):
        terms(mixed, go, 0, r, 0)

    def down(r):
        reduce_gone(r, 0)
        terms(hidden, gf, 1024, r, 1)

    def act(step, r):
        step(xm, r * S, S, 1 + r)

    exchanged(gq, 0, 0, WIDE)
    start_q()
    end_swap()
    gather_start(xg, 0, TOK, 0)
    exchanged(go, 1, 0, 512)
    exchanged(gf, 2, 0, 1536)
    early_q(0)
    early_q(1)
    early_q(2)
    early_q(3)
    gather_near(xg, 0, TOK, 0)
    early_q(4)
    early_q(5)
    start_o()
    late_q(0)
    gather_far(xg, 0, TOK, 0)
    late_q(1)
    gather_core(xg, 0, TOK, 0)
    scales(xg, 0)
    late_q(2)
    scales(xg, S)
    late_q(3)
    last_q(0)
    project(0)
    early_o(0)
    early_o(1)
    early_o(2)
    early_o(3)
    last_q(1)
    project(1)
    early_o(4)
    early_o(5)
    last_q(2)
    project(2)
    late_o(0)
    late_o(1)
    late_o(2)
    late_o(3)
    start_g()
    last_q(3)
    project(3)
    retention(0)
    last_o(0)
    last_o(1)
    last_o(2)
    last_o(3)
    out(0)
    early_g(0)
    early_g(1)
    early_g(2)
    early_g(3)
    retention(1)
    out(1)
    reduce_start(0, 0)
    early_g(4)
    early_g(5)
    reduce_start(1, 0)
    reduce_relay(0, 0)
    late_g(0)
    late_g(1)
    late_g(2)
    late_g(3)
    start_d()
    add_residual(0)
    act(gather_start, 0)
    reduce_relay(1, 0)
    early_d(0)
    early_d(1)
    early_d(2)
    early_d(3)
    add_residual(1)
    act(gather_start, 1)
    act(gather_near, 0)
    early_d(4)
    early_d(5)
    act(gather_far, 0)
    late_d(0)
    late_d(1)
    act(gather_near, 1)
    late_d(2)
    late_d(3)
    act(gather_core, 0)
    last_g(0)
    last_g(1)
    last_g(2)
    last_g(3)
    feed(0)
    act(gather_far, 1)
    act(gather_core, 1)
    feed(1)
    last_d(0)
    last_d(1)
    last_d(2)
    last_d(3)
    down(0)
    reduce_start(0, 1)
    down(1)
    serve_start()
    reduce_relay(0, 1)
    reduce_start(1, 1)
    finish(0)
    serve_end()
    reduce_relay(1, 1)
    save(0)
    finish(1)
    save(1)

    for group, (buf, lo, width) in enumerate(((gq, 0, WIDE), (go, 0, 512), (gf, 0, 1536))):
        gone(buf.at[0:112, lo : lo + width], group)
    gather_gone(xg, 0, TOK, 0)
    for r in range(REQS):
        act(gather_gone, r)
        reduce_gone(r, 1)
    left_q()
    left_o()
    left_g()
    left_d()

    @pl.when(source)
    def _():
        for i, srv in enumerate((srvq, srvo, srvf)):
            gone(srv, 11 + i)

    @pl.when(jnp.logical_not(source))
    def _():
        gone(hid, 3)
        for r in range(REQS):
            gone(outb.at[pl.ds(r * S, S), :], 22 + r)

    for one in stores():
        one.wait()
    saved(0)
    saved(1)


def settle(y_in, q_in, f_in, m_in, d_in, y, q, f, m, d, yv, qv, fv, mv, dv, sem):
    sets = ((y_in, yv, y), (q_in, qv, q), (f_in, fv, f), (m_in, mv, m), (d_in, dv, d))
    takes = [pltpu.make_async_copy(a, b, sem.at[i]) for i, (a, b, _) in enumerate(sets)]
    gives = [pltpu.make_async_copy(b, c, sem.at[5 + i]) for i, (_, b, c) in enumerate(sets)]
    for one in takes:
        one.start()
    for one, two in zip(takes, gives):
        one.wait()
        two.start()
    for one in gives:
        one.wait()


def layer(lengths, hidden, qkvg, gateup, out_t, down_t):
    cosine, sine = tables()
    hbm = pl.BlockSpec(memory_space=pl.ANY)
    dma = pltpu.SemaphoreType.DMA
    shapes = (
        jax.ShapeDtypeStruct((TOK, FEAT), BF),
        jax.ShapeDtypeStruct((128, WIDE), BF),
        jax.ShapeDtypeStruct((2, 128, 512), BF),
        jax.ShapeDtypeStruct((512, 128), BF),
        jax.ShapeDtypeStruct((512, 128), BF),
    )
    scratch = [
        pltpu.VMEM((16, HEADS * WIDE), F32),
        pltpu.VMEM((2, 16, FF), F32),
        pltpu.VMEM((16, HEADS * VAL), F32),
        pltpu.VMEM((16, FF), F32),
        pltpu.VMEM((S, KEY // 2), F32),
        pltpu.VMEM((S, KEY // 2), F32),
        pltpu.VMEM((2, 512, 128), BF),
        pltpu.VMEM((8, 16, WIDE), BF),
        pltpu.VMEM((8, 16, 512), BF),
        pltpu.VMEM((8, 16, 1536), BF),
        pltpu.VMEM((128, WIDE), BF),
        pltpu.VMEM((128, 512), BF),
        pltpu.VMEM((128, 1536), BF),
        pltpu.VMEM((TOK, D), BF),
        pltpu.VMEM((TOK, D), BF),
        pltpu.VMEM((D, WIDE), BF),
        pltpu.VMEM((D, 512), BF),
        pltpu.VMEM((D, 1536), BF),
        pltpu.VMEM((TOK, WIDE), F32),
        pltpu.VMEM((TOK, 128), F32),
        pltpu.VMEM((BLOCK, BLOCK), F32),
        pltpu.VMEM((BLOCK, BLOCK), F32),
        pltpu.VMEM((S, KEY), BF),
        pltpu.VMEM((S, KEY), BF),
        pltpu.VMEM((TOK, VAL), BF),
        pltpu.VMEM((TOK, 512), BF),
        pltpu.VMEM((REQS, 8, S, FEAT), BF),
        pltpu.VMEM((2, REQS, 4, S, FEAT), BF),
        pltpu.VMEM((2, REQS, 2, S // 2, FEAT), BF),
        pltpu.VMEM((2, REQS, 2, S, FEAT), BF),
        pltpu.VMEM((TOK, FEAT), F32),
        pltpu.VMEM((TOK, FEAT), BF),
        pltpu.VMEM((TOK, FEAT), BF),
        dma((24,)),
        dma((3,)),
        dma((3,)),
        dma((76,)),
        dma((12,)),
        dma((16,)),
        dma((8,)),
        dma((4,)),
        dma((3,)),
        dma((14,)),
    ]
    results = pl.pallas_call(
        kernel,
        out_shape=shapes,
        in_specs=[pl.BlockSpec(memory_space=pltpu.SMEM)] + [hbm] * 7,
        out_specs=(hbm,) * 5,
        scratch_shapes=scratch,
        compiler_params=pltpu.CompilerParams(
            collective_id=0, has_side_effects=True, vmem_limit_bytes=62 * 1024 * 1024
        ),
    )(lengths, hidden, qkvg, gateup, out_t, down_t, jnp.asarray(cosine), jnp.asarray(sine))
    return pl.pallas_call(
        settle,
        out_shape=shapes,
        in_specs=[hbm] * 5,
        out_specs=(hbm,) * 5,
        scratch_shapes=[pltpu.VMEM(one.shape, one.dtype) for one in shapes] + [dma((10,))],
    )(*results)


def shards(hidden_states, lengths, qkvg_master, gateup_master, out_master, down_master):
    return layer(
        lengths, hidden_states, qkvg_master, gateup_master, out_master.T, down_master.T
    )


def solution(mesh):
    return jax.shard_map(
        shards,
        mesh=mesh,
        in_specs=(
            P("row", "col"),
            P("row"),
            P(("row", "col"), None),
            P(None, ("row", "col"), None),
            P(None, ("row", "col")),
            P(None, ("row", "col")),
        ),
        out_specs=(
            P("row", "col"),
            P("row", "col"),
            P(None, "row", "col"),
            P("col", "row"),
            P("col", "row"),
        ),
        check_vma=False,
    )
```

```python
import math

import jax
import jax.numpy as jnp
import numpy as np
from jax import lax
from jax.experimental import pallas as pl
from jax.experimental.pallas import tpu as pltpu
from jax.sharding import PartitionSpec as P

D = 2048
HEADS = 8
KEY = 256
VAL = 512
S = 512
BLOCK = 256
FF = 4096
WIDE = 2 * KEY + 2 * VAL
TOK = 1024
FEAT = 256
REQS = 2
EPS = 1e-05
MESH = pl.DeviceIdType.MESH
BF = jnp.bfloat16
F32 = jnp.float32
NT = (((1,), (1,)), ((), ()))


def tables():
    half = KEY // 2
    freq = np.power(np.float32(10000.0), (-2.0 * np.arange(half) / KEY).astype(np.float32))
    angle = np.arange(S, dtype=np.float32)[:, None] * freq.astype(np.float32)[None, :]
    return np.cos(angle).astype(np.float32), np.sin(angle).astype(np.float32)


def kernel(
    lens, hid, qm_hbm, gm_hbm, om_hbm, dm_hbm, cos_hbm, sin_hbm,
    y, oq, of, om_out, od_out,
    qm, gm, om, dm, cosr, sinr, turned,
    sbq, sbo, sbf, srvq, srvo, srvf,
    xg, xm, gq, go, gf, acc, scl, near, far, qs, ks, mixed, hidden,
    part, pairs, relay, final, resid, outb, swapb,
    send_sem, sem_a2a, sem_own, sem_w, sem_x, sem_core, sem_rel, sem_fin, sem_swap, loc_sem,
):
    row = lax.axis_index("row")
    col = lax.axis_index("col")
    x = lax.div(row, 4)
    u = lax.rem(lax.div(row, 2), 2)
    c = lax.rem(row, 2)
    h = lax.div(col, 4)
    z = lax.rem(col, 4)
    xp, xn, xo = lax.rem(x + 1, 4), lax.rem(x + 3, 4), lax.rem(x + 2, 4)
    zp, zn, zo = lax.rem(z + 1, 4), lax.rem(z + 3, 4), lax.rem(z + 2, 4)
    source = c == h
    mine = c * 4 + z
    yy = h * 2 + u
    yp, yn, yo = lax.rem(yy + 1, 4), lax.rem(yy + 3, 4), lax.rem(yy + 2, 4)

    def device(xx, uu, cc, hh, zz):
        return (xx * 4 + uu * 2 + cc, hh * 4 + zz)

    to_core = device(x, u, 1 - c, h, z)
    to_swap = device(x, u, h, c, z)
    to_xp, to_xn = device(xp, u, c, h, z), device(xn, u, c, h, z)
    to_zp, to_zn = device(x, u, c, h, zp), device(x, u, c, h, zn)
    to_yp = device(x, lax.rem(yp, 2), c, lax.div(yp, 2), z)
    to_yn = device(x, lax.rem(yn, 2), c, lax.div(yn, 2), z)

    def post(src, dst, sent, recv, target):
        pltpu.make_async_remote_copy(
            src_ref=src,
            dst_ref=dst,
            send_sem=send_sem.at[sent],
            recv_sem=recv,
            device_id=target,
            device_id_type=MESH,
        ).start()

    def arrived(ref, recv):
        pltpu.make_async_remote_copy(
            src_ref=ref,
            dst_ref=ref,
            send_sem=send_sem.at[0],
            recv_sem=recv,
            device_id=to_core,
            device_id_type=MESH,
        ).wait_recv()

    def gone(ref, sent):
        pltpu.make_async_remote_copy(
            src_ref=ref,
            dst_ref=ref,
            send_sem=send_sem.at[sent],
            recv_sem=sem_swap.at[0],
            device_id=to_core,
            device_id_type=MESH,
        ).wait_send()

    loads = [
        pltpu.make_async_copy(src, dst, loc_sem.at[i])
        for i, (src, dst) in enumerate(
            ((qm_hbm, qm), (om_hbm, om), (gm_hbm, gm), (dm_hbm, dm), (cos_hbm, cosr), (sin_hbm, sinr))
        )
    ]
    for one in loads:
        one.start()

    barrier = pltpu.get_barrier_semaphore()
    others = [lax.rem(mine + i, 8) for i in range(1, 8)]
    peers = [device(x, u, lax.div(other, 4), h, lax.rem(other, 4)) for other in others]
    swap_peer = device(x, u, 1 - c, 1 - h, z)
    greet = peers + [swap_peer, to_xp, to_xn, to_yp, to_yn]
    for peer in greet:
        pl.semaphore_signal(barrier, inc=1, device_id=peer, device_id_type=MESH)
    loads[0].wait()
    for i in range(8):
        sbq[i] = qm[:, i * WIDE : (i + 1) * WIDE].astype(BF)
    pl.semaphore_wait(barrier, len(greet))

    def dealt(buf, cc, zz, lo, width):
        start = (x * 4 + u * 2 + cc) * 128 + h * 64 + zz * 16
        return buf.at[pl.ds(pl.multiple_of(start, 16), 16), pl.ds(lo, width)]

    def exchange(send, buf, group, lo, width):
        for i in range(1, 8):
            other = lax.rem(mine + i, 8)
            post(
                send.at[other],
                dealt(buf, c, z, lo, width),
                group,
                sem_a2a.at[group],
                device(x, u, lax.div(other, 4), h, lax.rem(other, 4)),
            )
        start = (x * 4 + u * 2 + c) * 128 + h * 64 + z * 16
        buf[pl.ds(pl.multiple_of(start, 16), 16), lo : lo + width] = send[mine]

    def exchanged(buf, group, lo, width):
        arrived(buf.at[0:112, lo : lo + width], sem_a2a.at[group])

    exchange(sbq, gq, 0, 0, WIDE)

    def lanes(slot):
        return pl.ds(pl.multiple_of(slot * FEAT, FEAT), FEAT)

    def start_swap():
        @pl.when(jnp.logical_not(source))
        def _():
            post(hid, xg.at[:, lanes(col)], 3, sem_swap.at[0], to_swap)

        @pl.when(source)
        def _():
            pltpu.make_async_copy(hid, xg.at[:, lanes(col)], loc_sem.at[6]).start()

    def end_swap():
        @pl.when(jnp.logical_not(source))
        def _():
            arrived(xg.at[:, lanes(mine)], sem_swap.at[0])

        @pl.when(source)
        def _():
            pltpu.make_async_copy(hid, xg.at[:, lanes(col)], loc_sem.at[6]).wait()

    start_swap()

    for one in loads[1:]:
        one.wait()
    for i in range(8):
        sbo[i] = om[:, i * VAL : (i + 1) * VAL].astype(BF)
        sbf[i, :, 0:512] = gm[0, :, i * 512 : (i + 1) * 512].astype(BF)
        sbf[i, :, 512:1024] = gm[1, :, i * 512 : (i + 1) * 512].astype(BF)
        sbf[i, :, 1024:1536] = dm[:, i * 512 : (i + 1) * 512].astype(BF)
    exchange(sbo, go, 1, 0, 512)
    exchange(sbf, gf, 2, 0, 1536)

    head = c * 4 + z
    rate = jnp.float32(0.0)
    for i in range(HEADS):
        rate = jnp.where(head == i, jnp.float32(math.log1p(-(2.0 ** (-5 - i)))), rate)
    lag = lax.broadcasted_iota(jnp.int32, (BLOCK, BLOCK), 0) - lax.broadcasted_iota(
        jnp.int32, (BLOCK, BLOCK), 1
    )
    near[...] = jnp.where(lag >= 0, jnp.exp(jnp.maximum(lag, 0).astype(F32) * rate), 0.0)
    far[...] = jnp.exp((lag + BLOCK).astype(F32) * rate)

    def act_ref(buf, rows, slot):
        return buf.at[rows, lanes(slot)]

    def gather_post(buf, rows, slot, bank, kind, to):
        ref = act_ref(buf, rows, slot)
        post(ref, ref, 4 + bank, sem_x.at[bank * 4 + kind], to)

    def gather_start(buf, first, size, bank):
        rows = pl.ds(first, size)
        gather_post(buf, rows, mine, bank, 0, to_zp)
        gather_post(buf, rows, mine, bank, 1, to_zn)
        gather_post(buf, rows, mine, bank, 3, to_core)

    def gather_near(buf, first, size, bank):
        rows = pl.ds(first, size)
        half = size // 2
        for kind, zz, start, to in ((0, zn, first, to_zp), (1, zp, first + half, to_zn)):
            slot = c * 4 + zz
            arrived(act_ref(buf, rows, slot), sem_x.at[bank * 4 + kind])
            gather_post(buf, pl.ds(start, half), slot, bank, 2, to)
            gather_post(buf, rows, slot, bank, 3, to_core)

    def gather_far(buf, first, size, bank):
        rows = pl.ds(first, size)
        slot = c * 4 + zo
        arrived(act_ref(buf, rows, slot), sem_x.at[bank * 4 + 2])
        gather_post(buf, rows, slot, bank, 3, to_core)

    def gather_core(buf, first, size, bank):
        theirs = pl.ds(pl.multiple_of((1 - c) * 1024, 1024), 1024)
        arrived(buf.at[pl.ds(first, size), theirs], sem_x.at[bank * 4 + 3])

    def gather_gone(buf, first, size, bank):
        gone(buf.at[pl.ds(first, size), 0 : 7 * FEAT], 4 + bank)

    def weights(buf, bank, lo, width):
        xs, ys = (x, xn, xp, xo), (yy, yn, yp, yo)
        cut = pl.ds(lo, width)

        def block(key, half=None):
            xx, where, cc = key
            start = (xx * 4 + lax.rem(where, 2) * 2 + cc) * 128 + lax.div(where, 2) * 64
            if half is None:
                return buf.at[pl.ds(pl.multiple_of(start, 64), 64), cut]
            return buf.at[pl.ds(pl.multiple_of(start + half * 32, 32), 32), cut]

        def send(key, to, kind, half=None):
            ref = block(key, half)
            post(ref, ref, 7 + bank, sem_w.at[bank * 19 + kind], to)

        def wait(key, kind):
            arrived(block(key), sem_w.at[bank * 19 + kind])

        def start():
            for to, kind in ((to_xp, 0), (to_xn, 2), (to_yp, 6), (to_yn, 6)):
                send((x, yy, 0), to, kind)
            for to, kind in ((to_yp, 1), (to_yn, 3), (to_xp, 10), (to_xn, 10)):
                send((x, yy, 1), to, kind)

        def early(i):
            key = (
                (xn, yy, 0), (x, yn, 1), (xp, yy, 0), (x, yp, 1), (xo, yy, 0), (x, yo, 1)
            )[i]
            wait(key, i)
            if i < 4:
                send(key, (to_xp, to_yp, to_xn, to_yn)[i], 4 + i % 2, i // 2)
            place = i // 2 + 1
            if i % 2 == 0:
                send(key, to_yp, 6 + place)
                send(key, to_yn, 6 + place)
            else:
                send(key, to_xp, 10 + place)
                send(key, to_xn, 10 + place)

        def late(i):
            arrived(buf.at[0:128, cut], sem_w.at[bank * 19 + 6 + i])
            if i in (0, 3):
                send((xs[i], yn, 0), to_yp, 14 + i)
            else:
                send((xs[i], yp, 0), to_yn, 14 + i)
            arrived(buf.at[0:128, cut], sem_w.at[bank * 19 + 10 + i])
            if i in (0, 3):
                send((xn, ys[i], 1), to_xp, 18)
            else:
                send((xp, ys[i], 1), to_xn, 18)

        def last(i):
            wait((xs[i], yo, 0), 14 + i)
            if i == 3:
                arrived(buf.at[0:256, cut], sem_w.at[bank * 19 + 18])

        def left():
            gone(buf.at[0:1920, cut], 7 + bank)

        return start, early, late, last, left

    start_q, early_q, late_q, last_q, left_q = weights(gq, 0, 0, WIDE)
    start_o, early_o, late_o, last_o, left_o = weights(go, 1, 0, 512)
    start_g, early_g, late_g, last_g, left_g = weights(gf, 2, 0, 1024)
    start_d, early_d, late_d, last_d, left_d = weights(gf, 3, 1024, 512)

    def serve_start():
        theirs = pl.ds(pl.multiple_of((x * 4 + u * 2 + 1 - c) * 128, 128), 128)
        ours = pl.ds(pl.multiple_of(row * 128, 128), 128)

        @pl.when(source)
        def _():
            for i, (buf, srv) in enumerate(((gq, srvq), (go, srvo), (gf, srvf))):
                post(buf.at[theirs, :], srv, 11 + i, sem_own.at[i], to_core)
                srv[...] = buf[ours, :]

    def serve_end():
        @pl.when(jnp.logical_not(source))
        def _():
            for i, srv in enumerate((srvq, srvo, srvf)):
                arrived(srv, sem_own.at[i])

        store_weights()

    def stores():
        return [
            pltpu.make_async_copy(srvq, oq, loc_sem.at[7]),
            pltpu.make_async_copy(srvf.at[:, 0:512], of.at[0], loc_sem.at[8]),
            pltpu.make_async_copy(srvf.at[:, 512:1024], of.at[1], loc_sem.at[9]),
            pltpu.make_async_copy(turned.at[0], om_out, loc_sem.at[10]),
            pltpu.make_async_copy(turned.at[1], od_out, loc_sem.at[11]),
        ]

    def store_weights():
        turned[0] = jnp.transpose(srvo[...])
        turned[1] = jnp.transpose(srvf[:, 1024:1536])
        for one in stores():
            one.start()

    def scales(buf, first):
        @pl.loop(0, S // 128)
        def _(i):
            rows = pl.ds(pl.multiple_of(first + i * 128, 128), 128)
            tokens = buf[rows, :].astype(F32)
            total = jnp.sum(tokens * tokens, axis=1, keepdims=True)
            scl[rows, :] = jnp.broadcast_to(lax.rsqrt(total * (1.0 / D) + EPS), (128, 128))

    def project(i):
        feats = pl.ds(pl.multiple_of((x, xn, xp, xo)[i] * 512, 512), 512)

        @pl.loop(0, WIDE // 256)
        def _(n):
            wide = pl.ds(pl.multiple_of(n * 256, 256), 256)
            for m in range(REQS):
                rows = pl.ds(m * S, S)
                term = jnp.dot(xg[rows, feats], gq[feats, wide], preferred_element_type=F32)
                if i == 0:
                    acc[rows, wide] = term
                else:
                    acc[rows, wide] += term

    def retention(r):
        first = r * S
        rows = pl.ds(first, S)
        scale = scl[rows, :]
        for ref, at, gain in ((qs, 0, 1.0), (ks, KEY, 1.0 / math.sqrt(KEY))):
            a = (acc[rows, at : at + 128] * scale).astype(BF).astype(F32)
            b = (acc[rows, at + 128 : at + 256] * scale).astype(BF).astype(F32)
            ref[:, 0:128] = ((a * cosr[...] - b * sinr[...]) * gain).astype(BF)
            ref[:, 128:256] = ((a * sinr[...] + b * cosr[...]) * gain).astype(BF)
        wide_scale = jnp.concatenate([scale] * 4, axis=1)
        value = (acc[rows, 512:1024] * wide_scale).astype(BF)
        for t in range(S // BLOCK):
            q = qs[t * BLOCK : (t + 1) * BLOCK, :]
            total = jnp.zeros((BLOCK, VAL), F32)
            denom = jnp.zeros((BLOCK, 1), F32)
            for s in range(t + 1):
                k = ks[s * BLOCK : (s + 1) * BLOCK, :]
                score = lax.dot_general(q, k, NT, preferred_element_type=F32)
                score = score * (near[...] if s == t else far[...])
                denom += jnp.sum(score, axis=1, keepdims=True)
                total += jnp.dot(
                    score.astype(BF),
                    value[s * BLOCK : (s + 1) * BLOCK, :],
                    preferred_element_type=F32,
                )
            kept = total / jnp.maximum(jnp.abs(denom), 1.0)
            centred = kept - jnp.mean(kept, axis=1, keepdims=True)
            spread = jnp.mean(centred * centred, axis=1, keepdims=True)
            block = pl.ds(first + t * BLOCK, BLOCK)
            gate = (acc[block, 1024:1536] * wide_scale[t * BLOCK : (t + 1) * BLOCK, :]).astype(BF)
            mixed[block, :] = (
                jax.nn.silu(gate.astype(F32)) * (centred * lax.rsqrt(spread + EPS))
            ).astype(BF)

    def terms(left, weight, at, r, bank):
        rows = pl.ds(r * S, S)

        def term(slot):
            feats = pl.ds(pl.multiple_of(slot * FEAT, FEAT), FEAT)
            part[r, slot] = lax.dot_general(
                left[rows, :], weight[feats, at : at + 512], NT, preferred_element_type=F32
            ).astype(BF)

        @pl.loop(0, 4)
        def _(j):
            zz = lax.rem(zo + j, 4)
            slot = (1 - c) * 4 + zz
            term(slot)
            post(
                part.at[r, slot],
                pairs.at[bank, r, zz],
                14 + bank * 2 + r,
                sem_core.at[bank * 8 + r * 4 + zz],
                to_core,
            )

        @pl.loop(0, 4)
        def _(j):
            term(c * 4 + lax.rem(zo + j, 4))

    HALF = S // 2
    TOP, BOT = pl.ds(0, HALF), pl.ds(HALF, HALF)

    def pair(r, bank, zz):
        arrived(pairs.at[bank, r, zz], sem_core.at[bank * 8 + r * 4 + zz])
        slot = c * 4 + zz
        return slot

    def both(r, bank, zz, rows):
        return part[r, c * 4 + zz, rows, :].astype(F32) + pairs[bank, r, zz, rows, :].astype(F32)

    def reduce_start(r, bank):
        rel = (bank * 2 + r) * 2
        slot = pair(r, bank, zo)
        part[r, slot] = both(r, bank, zo, pl.ds(0, S)).astype(BF)
        post(part.at[r, slot, TOP, :], relay.at[bank, r, 0], 18 + bank * 2 + r, sem_rel.at[rel], to_zp)
        post(part.at[r, slot, BOT, :], relay.at[bank, r, 1], 18 + bank * 2 + r, sem_rel.at[rel + 1], to_zn)
        slot = pair(r, bank, zp)
        part[r, slot, BOT, :] = both(r, bank, zp, BOT).astype(BF)
        post(part.at[r, slot, BOT, :], final.at[bank, r, 0, BOT, :], 18 + bank * 2 + r, sem_fin.at[bank * 2 + r], to_zp)
        slot = pair(r, bank, zn)
        part[r, slot, TOP, :] = both(r, bank, zn, TOP).astype(BF)
        post(part.at[r, slot, TOP, :], final.at[bank, r, 1, TOP, :], 18 + bank * 2 + r, sem_fin.at[bank * 2 + r], to_zn)

    def reduce_relay(r, bank):
        rel = (bank * 2 + r) * 2
        arrived(relay.at[bank, r, 0], sem_rel.at[rel])
        slot = c * 4 + zp
        part[r, slot, TOP, :] = (both(r, bank, zp, TOP) + relay[bank, r, 0].astype(F32)).astype(BF)
        post(part.at[r, slot, TOP, :], final.at[bank, r, 0, TOP, :], 18 + bank * 2 + r, sem_fin.at[bank * 2 + r], to_zp)
        arrived(relay.at[bank, r, 1], sem_rel.at[rel + 1])
        slot = c * 4 + zn
        part[r, slot, BOT, :] = (both(r, bank, zn, BOT) + relay[bank, r, 1].astype(F32)).astype(BF)
        post(part.at[r, slot, BOT, :], final.at[bank, r, 1, BOT, :], 18 + bank * 2 + r, sem_fin.at[bank * 2 + r], to_zn)
        pair(r, bank, z)

    def reduce_end(r, bank):
        arrived(final.at[bank, r], sem_fin.at[bank * 2 + r])
        return (
            both(r, bank, z, pl.ds(0, S))
            + final[bank, r, 0].astype(F32)
            + final[bank, r, 1].astype(F32)
        )

    def reduce_gone(r, bank):
        gone(part.at[r, 0:4], 14 + bank * 2 + r)
        gone(part.at[r, 0:3], 18 + bank * 2 + r)

    def add_residual(r):
        rows = pl.ds(r * S, S)
        total = xg[rows, lanes(mine)].astype(F32) + reduce_end(r, 0)
        resid[rows, :] = total
        xm[rows, lanes(mine)] = total.astype(BF)

    def feed(r):
        rows = pl.ds(r * S, S)
        scales(xm, r * S)
        scale = jnp.concatenate([scl[rows, :]] * 2, axis=1)

        @pl.loop(0, 2)
        def _(n):
            at = pl.ds(pl.multiple_of(n * 256, 256), 256)
            up_at = pl.ds(pl.multiple_of(512 + n * 256, 256), 256)
            gate = jnp.dot(xm[rows, :], gf[:, at], preferred_element_type=F32) * scale
            up = jnp.dot(xm[rows, :], gf[:, up_at], preferred_element_type=F32) * scale
            hidden[rows, at] = (jax.nn.silu(gate) * up).astype(BF)

    def finish(r):
        rows = pl.ds(r * S, S)
        outb[rows, :] = (resid[rows, :] + reduce_end(r, 1)).astype(BF)

        @pl.when(jnp.logical_not(source))
        def _():
            post(outb.at[rows, :], swapb.at[rows, :], 22 + r, sem_swap.at[1 + r], to_swap)

    def save(r):
        rows = pl.ds(r * S, S)
        live = lax.broadcasted_iota(jnp.int32, (S, FEAT), 0) < lens[r]

        @pl.when(source)
        def _():
            swapb[rows, :] = jnp.where(live, outb[rows, :], jnp.zeros((S, FEAT), BF))

        @pl.when(jnp.logical_not(source))
        def _():
            arrived(swapb.at[rows, :], sem_swap.at[1 + r])
            swapb[rows, :] = jnp.where(live, swapb[rows, :], jnp.zeros((S, FEAT), BF))

        pltpu.make_async_copy(swapb.at[rows, :], y.at[rows, :], loc_sem.at[12 + r]).start()

    def saved(r):
        rows = pl.ds(r * S, S)
        pltpu.make_async_copy(swapb.at[rows, :], y.at[rows, :], loc_sem.at[12 + r]).wait()

    def out(r):
        terms(mixed, go, 0, r, 0)

    def down(r):
        reduce_gone(r, 0)
        terms(hidden, gf, 1024, r, 1)

    def act(step, r):
        step(xm, r * S, S, 1 + r)

    exchanged(gq, 0, 0, WIDE)
    start_q()
    end_swap()
    gather_start(xg, 0, TOK, 0)
    exchanged(go, 1, 0, 512)
    start_o()
    exchanged(gf, 2, 0, 1536)
    early_q(0)
    early_q(1)
    early_q(2)
    early_q(3)
    early_o(0)
    early_o(1)
    early_o(2)
    early_o(3)
    gather_near(xg, 0, TOK, 0)
    early_q(4)
    early_q(5)
    early_o(4)
    early_o(5)
    late_q(0)
    late_o(0)
    gather_far(xg, 0, TOK, 0)
    late_q(1)
    late_o(1)
    gather_core(xg, 0, TOK, 0)
    scales(xg, 0)
    late_q(2)
    late_o(2)
    scales(xg, S)
    late_q(3)
    late_o(3)
    start_g()
    last_q(0)
    project(0)
    last_q(1)
    project(1)
    last_q(2)
    project(2)
    last_q(3)
    project(3)
    early_g(0)
    early_g(1)
    retention(0)
    last_o(0)
    last_o(1)
    last_o(2)
    last_o(3)
    out(0)
    reduce_start(0, 0)
    early_g(2)
    early_g(3)
    early_g(4)
    early_g(5)
    start_d()
    retention(1)
    late_g(0)
    late_g(1)
    reduce_relay(0, 0)
    out(1)
    reduce_start(1, 0)
    late_g(2)
    late_g(3)
    early_d(0)
    early_d(1)
    early_d(2)
    early_d(3)
    add_residual(0)
    act(gather_start, 0)
    reduce_relay(1, 0)
    early_d(4)
    early_d(5)
    act(gather_near, 0)
    add_residual(1)
    act(gather_start, 1)
    late_d(0)
    late_d(1)
    act(gather_far, 0)
    act(gather_near, 1)
    late_d(2)
    late_d(3)
    act(gather_core, 0)
    last_g(0)
    last_g(1)
    last_g(2)
    last_g(3)
    feed(0)
    last_d(0)
    last_d(1)
    last_d(2)
    last_d(3)
    down(0)
    reduce_start(0, 1)
    act(gather_far, 1)
    act(gather_core, 1)
    feed(1)
    reduce_relay(0, 1)
    down(1)
    reduce_start(1, 1)
    finish(0)
    serve_start()
    reduce_relay(1, 1)
    save(0)
    serve_end()
    finish(1)
    save(1)

    for group, (buf, lo, width) in enumerate(((gq, 0, WIDE), (go, 0, 512), (gf, 0, 1536))):
        gone(buf.at[0:112, lo : lo + width], group)
    gather_gone(xg, 0, TOK, 0)
    for r in range(REQS):
        act(gather_gone, r)
        reduce_gone(r, 1)
    left_q()
    left_o()
    left_g()
    left_d()

    @pl.when(source)
    def _():
        for i, srv in enumerate((srvq, srvo, srvf)):
            gone(srv, 11 + i)

    @pl.when(jnp.logical_not(source))
    def _():
        gone(hid, 3)
        for r in range(REQS):
            gone(outb.at[pl.ds(r * S, S), :], 22 + r)

    for one in stores():
        one.wait()
    saved(0)
    saved(1)


def settle(y_in, q_in, f_in, m_in, d_in, y, q, f, m, d, yv, qv, fv, mv, dv, sem):
    sets = ((y_in, yv, y), (q_in, qv, q), (f_in, fv, f), (m_in, mv, m), (d_in, dv, d))
    takes = [pltpu.make_async_copy(a, b, sem.at[i]) for i, (a, b, _) in enumerate(sets)]
    gives = [pltpu.make_async_copy(b, c, sem.at[5 + i]) for i, (_, b, c) in enumerate(sets)]
    for one in takes:
        one.start()
    for one, two in zip(takes, gives):
        one.wait()
        two.start()
    for one in gives:
        one.wait()


def layer(lengths, hidden, qkvg, gateup, out_t, down_t):
    cosine, sine = tables()
    hbm = pl.BlockSpec(memory_space=pl.ANY)
    dma = pltpu.SemaphoreType.DMA
    shapes = (
        jax.ShapeDtypeStruct((TOK, FEAT), BF),
        jax.ShapeDtypeStruct((128, WIDE), BF),
        jax.ShapeDtypeStruct((2, 128, 512), BF),
        jax.ShapeDtypeStruct((512, 128), BF),
        jax.ShapeDtypeStruct((512, 128), BF),
    )
    scratch = [
        pltpu.VMEM((16, HEADS * WIDE), F32),
        pltpu.VMEM((2, 16, FF), F32),
        pltpu.VMEM((16, HEADS * VAL), F32),
        pltpu.VMEM((16, FF), F32),
        pltpu.VMEM((S, KEY // 2), F32),
        pltpu.VMEM((S, KEY // 2), F32),
        pltpu.VMEM((2, 512, 128), BF),
        pltpu.VMEM((8, 16, WIDE), BF),
        pltpu.VMEM((8, 16, 512), BF),
        pltpu.VMEM((8, 16, 1536), BF),
        pltpu.VMEM((128, WIDE), BF),
        pltpu.VMEM((128, 512), BF),
        pltpu.VMEM((128, 1536), BF),
        pltpu.VMEM((TOK, D), BF),
        pltpu.VMEM((TOK, D), BF),
        pltpu.VMEM((D, WIDE), BF),
        pltpu.VMEM((D, 512), BF),
        pltpu.VMEM((D, 1536), BF),
        pltpu.VMEM((TOK, WIDE), F32),
        pltpu.VMEM((TOK, 128), F32),
        pltpu.VMEM((BLOCK, BLOCK), F32),
        pltpu.VMEM((BLOCK, BLOCK), F32),
        pltpu.VMEM((S, KEY), BF),
        pltpu.VMEM((S, KEY), BF),
        pltpu.VMEM((TOK, VAL), BF),
        pltpu.VMEM((TOK, 512), BF),
        pltpu.VMEM((REQS, 8, S, FEAT), BF),
        pltpu.VMEM((2, REQS, 4, S, FEAT), BF),
        pltpu.VMEM((2, REQS, 2, S // 2, FEAT), BF),
        pltpu.VMEM((2, REQS, 2, S, FEAT), BF),
        pltpu.VMEM((TOK, FEAT), F32),
        pltpu.VMEM((TOK, FEAT), BF),
        pltpu.VMEM((TOK, FEAT), BF),
        dma((24,)),
        dma((3,)),
        dma((3,)),
        dma((76,)),
        dma((12,)),
        dma((16,)),
        dma((8,)),
        dma((4,)),
        dma((3,)),
        dma((14,)),
    ]
    results = pl.pallas_call(
        kernel,
        out_shape=shapes,
        in_specs=[pl.BlockSpec(memory_space=pltpu.SMEM)] + [hbm] * 7,
        out_specs=(hbm,) * 5,
        scratch_shapes=scratch,
        compiler_params=pltpu.CompilerParams(
            collective_id=0, has_side_effects=True, vmem_limit_bytes=62 * 1024 * 1024
        ),
    )(lengths, hidden, qkvg, gateup, out_t, down_t, jnp.asarray(cosine), jnp.asarray(sine))
    return pl.pallas_call(
        settle,
        out_shape=shapes,
        in_specs=[hbm] * 5,
        out_specs=(hbm,) * 5,
        scratch_shapes=[pltpu.VMEM(one.shape, one.dtype) for one in shapes] + [dma((10,))],
    )(*results)


def shards(hidden_states, lengths, qkvg_master, gateup_master, out_master, down_master):
    return layer(
        lengths, hidden_states, qkvg_master, gateup_master, out_master.T, down_master.T
    )


def solution(mesh):
    return jax.shard_map(
        shards,
        mesh=mesh,
        in_specs=(
            P("row", "col"),
            P("row"),
            P(("row", "col"), None),
            P(None, ("row", "col"), None),
            P(None, ("row", "col")),
            P(None, ("row", "col")),
        ),
        out_specs=(
            P("row", "col"),
            P("row", "col"),
            P(None, "row", "col"),
            P("col", "row"),
            P("col", "row"),
        ),
        check_vma=False,
    )
```

```python
import math

import jax
import jax.numpy as jnp
import numpy as np
from jax import lax
from jax.experimental import pallas as pl
from jax.experimental.pallas import tpu as pltpu
from jax.sharding import PartitionSpec as P

D = 2048
HEADS = 8
KEY = 256
VAL = 512
S = 512
BLOCK = 256
FF = 4096
WIDE = 2 * KEY + 2 * VAL
TOK = 1024
FEAT = 256
REQS = 2
EPS = 1e-05
MESH = pl.DeviceIdType.MESH
BF = jnp.bfloat16
F32 = jnp.float32
NT = (((1,), (1,)), ((), ()))


def tables():
    half = KEY // 2
    freq = np.power(np.float32(10000.0), (-2.0 * np.arange(half) / KEY).astype(np.float32))
    angle = np.arange(S, dtype=np.float32)[:, None] * freq.astype(np.float32)[None, :]
    return np.cos(angle).astype(np.float32), np.sin(angle).astype(np.float32)


def kernel(
    lens, hid, qm_hbm, gm_hbm, om_hbm, dm_hbm, cos_hbm, sin_hbm,
    y, oq, of, om_out, od_out,
    qm, gm, om, dm, cosr, sinr, turned,
    sbq, sbo, sbf, srvq, srvo, srvf,
    xg, xm, gq, go, gf, acc, scl, near, far, qs, ks, mixed, hidden,
    part, pairs, relay, final, resid, outb, swapb,
    send_sem, sem_a2a, sem_own, sem_w, sem_x, sem_core, sem_rel, sem_fin, sem_swap, loc_sem,
):
    row = lax.axis_index("row")
    col = lax.axis_index("col")
    x = lax.div(row, 4)
    u = lax.rem(lax.div(row, 2), 2)
    c = lax.rem(row, 2)
    h = lax.div(col, 4)
    z = lax.rem(col, 4)
    xp, xn, xo = lax.rem(x + 1, 4), lax.rem(x + 3, 4), lax.rem(x + 2, 4)
    zp, zn, zo = lax.rem(z + 1, 4), lax.rem(z + 3, 4), lax.rem(z + 2, 4)
    source = c == h
    mine = c * 4 + z
    yy = h * 2 + u
    yp, yn, yo = lax.rem(yy + 1, 4), lax.rem(yy + 3, 4), lax.rem(yy + 2, 4)

    def device(xx, uu, cc, hh, zz):
        return (xx * 4 + uu * 2 + cc, hh * 4 + zz)

    to_core = device(x, u, 1 - c, h, z)
    to_swap = device(x, u, h, c, z)
    to_xp, to_xn = device(xp, u, c, h, z), device(xn, u, c, h, z)
    to_zp, to_zn = device(x, u, c, h, zp), device(x, u, c, h, zn)
    to_yp = device(x, lax.rem(yp, 2), c, lax.div(yp, 2), z)
    to_yn = device(x, lax.rem(yn, 2), c, lax.div(yn, 2), z)

    def post(src, dst, sent, recv, target):
        pltpu.make_async_remote_copy(
            src_ref=src,
            dst_ref=dst,
            send_sem=send_sem.at[sent],
            recv_sem=recv,
            device_id=target,
            device_id_type=MESH,
        ).start()

    def arrived(ref, recv):
        pltpu.make_async_remote_copy(
            src_ref=ref,
            dst_ref=ref,
            send_sem=send_sem.at[0],
            recv_sem=recv,
            device_id=to_core,
            device_id_type=MESH,
        ).wait_recv()

    def gone(ref, sent):
        pltpu.make_async_remote_copy(
            src_ref=ref,
            dst_ref=ref,
            send_sem=send_sem.at[sent],
            recv_sem=sem_swap.at[0],
            device_id=to_core,
            device_id_type=MESH,
        ).wait_send()

    loads = [
        pltpu.make_async_copy(src, dst, loc_sem.at[i])
        for i, (src, dst) in enumerate(
            ((qm_hbm, qm), (om_hbm, om), (gm_hbm, gm), (dm_hbm, dm), (cos_hbm, cosr), (sin_hbm, sinr))
        )
    ]
    for one in loads:
        one.start()

    barrier = pltpu.get_barrier_semaphore()
    others = [lax.rem(mine + i, 8) for i in range(1, 8)]
    peers = [device(x, u, lax.div(other, 4), h, lax.rem(other, 4)) for other in others]
    swap_peer = device(x, u, 1 - c, 1 - h, z)
    greet = peers + [swap_peer, to_xp, to_xn, to_yp, to_yn]
    for peer in greet:
        pl.semaphore_signal(barrier, inc=1, device_id=peer, device_id_type=MESH)
    loads[0].wait()
    for i in range(8):
        sbq[i] = qm[:, i * WIDE : (i + 1) * WIDE].astype(BF)
    pl.semaphore_wait(barrier, len(greet))

    def dealt(buf, cc, zz, lo, width):
        start = (x * 4 + u * 2 + cc) * 128 + h * 64 + zz * 16
        return buf.at[pl.ds(pl.multiple_of(start, 16), 16), pl.ds(lo, width)]

    def exchange(send, buf, group, lo, width):
        for i in range(1, 8):
            other = lax.rem(mine + i, 8)
            post(
                send.at[other],
                dealt(buf, c, z, lo, width),
                group,
                sem_a2a.at[group],
                device(x, u, lax.div(other, 4), h, lax.rem(other, 4)),
            )
        start = (x * 4 + u * 2 + c) * 128 + h * 64 + z * 16
        buf[pl.ds(pl.multiple_of(start, 16), 16), lo : lo + width] = send[mine]

    def exchanged(buf, group, lo, width):
        arrived(buf.at[0:112, lo : lo + width], sem_a2a.at[group])

    exchange(sbq, gq, 0, 0, WIDE)

    def lanes(slot):
        return pl.ds(pl.multiple_of(slot * FEAT, FEAT), FEAT)

    def start_swap():
        @pl.when(jnp.logical_not(source))
        def _():
            post(hid, xg.at[:, lanes(col)], 3, sem_swap.at[0], to_swap)

        @pl.when(source)
        def _():
            pltpu.make_async_copy(hid, xg.at[:, lanes(col)], loc_sem.at[6]).start()

    def end_swap():
        @pl.when(jnp.logical_not(source))
        def _():
            arrived(xg.at[:, lanes(mine)], sem_swap.at[0])

        @pl.when(source)
        def _():
            pltpu.make_async_copy(hid, xg.at[:, lanes(col)], loc_sem.at[6]).wait()

    start_swap()

    for one in loads[1:]:
        one.wait()
    for i in range(8):
        sbo[i] = om[:, i * VAL : (i + 1) * VAL].astype(BF)
    exchange(sbo, go, 1, 0, 512)

    def act_ref(buf, rows, slot):
        return buf.at[rows, lanes(slot)]

    def gather_post(buf, rows, slot, bank, kind, to):
        ref = act_ref(buf, rows, slot)
        post(ref, ref, 4 + bank, sem_x.at[bank * 4 + kind], to)

    def gather_start(buf, first, size, bank):
        rows = pl.ds(first, size)
        gather_post(buf, rows, mine, bank, 0, to_zp)
        gather_post(buf, rows, mine, bank, 1, to_zn)
        gather_post(buf, rows, mine, bank, 3, to_core)

    def gather_near(buf, first, size, bank):
        rows = pl.ds(first, size)
        half = size // 2
        for kind, zz, start, to in ((0, zn, first, to_zp), (1, zp, first + half, to_zn)):
            slot = c * 4 + zz
            arrived(act_ref(buf, rows, slot), sem_x.at[bank * 4 + kind])
            gather_post(buf, pl.ds(start, half), slot, bank, 2, to)
            gather_post(buf, rows, slot, bank, 3, to_core)

    def gather_far(buf, first, size, bank):
        rows = pl.ds(first, size)
        slot = c * 4 + zo
        arrived(act_ref(buf, rows, slot), sem_x.at[bank * 4 + 2])
        gather_post(buf, rows, slot, bank, 3, to_core)

    def gather_core(buf, first, size, bank):
        theirs = pl.ds(pl.multiple_of((1 - c) * 1024, 1024), 1024)
        arrived(buf.at[pl.ds(first, size), theirs], sem_x.at[bank * 4 + 3])

    def gather_gone(buf, first, size, bank):
        gone(buf.at[pl.ds(first, size), 0 : 7 * FEAT], 4 + bank)

    def weights(buf, bank, lo, width):
        xs, ys = (x, xn, xp, xo), (yy, yn, yp, yo)
        cut = pl.ds(lo, width)

        def block(key, half=None):
            xx, where, cc = key
            start = (xx * 4 + lax.rem(where, 2) * 2 + cc) * 128 + lax.div(where, 2) * 64
            if half is None:
                return buf.at[pl.ds(pl.multiple_of(start, 64), 64), cut]
            return buf.at[pl.ds(pl.multiple_of(start + half * 32, 32), 32), cut]

        def send(key, to, kind, half=None):
            ref = block(key, half)
            post(ref, ref, 7 + bank, sem_w.at[bank * 19 + kind], to)

        def wait(key, kind):
            arrived(block(key), sem_w.at[bank * 19 + kind])

        def start():
            for to, kind in ((to_xp, 0), (to_xn, 2), (to_yp, 6), (to_yn, 6)):
                send((x, yy, 0), to, kind)
            for to, kind in ((to_yp, 1), (to_yn, 3), (to_xp, 10), (to_xn, 10)):
                send((x, yy, 1), to, kind)

        def early(i):
            key = (
                (xn, yy, 0), (x, yn, 1), (xp, yy, 0), (x, yp, 1), (xo, yy, 0), (x, yo, 1)
            )[i]
            wait(key, i)
            if i < 4:
                send(key, (to_xp, to_yp, to_xn, to_yn)[i], 4 + i % 2, i // 2)
            place = i // 2 + 1
            if i % 2 == 0:
                send(key, to_yp, 6 + place)
                send(key, to_yn, 6 + place)
            else:
                send(key, to_xp, 10 + place)
                send(key, to_xn, 10 + place)

        def late(i):
            arrived(buf.at[0:128, cut], sem_w.at[bank * 19 + 6 + i])
            if i in (0, 3):
                send((xs[i], yn, 0), to_yp, 14 + i)
            else:
                send((xs[i], yp, 0), to_yn, 14 + i)
            arrived(buf.at[0:128, cut], sem_w.at[bank * 19 + 10 + i])
            if i in (0, 3):
                send((xn, ys[i], 1), to_xp, 18)
            else:
                send((xp, ys[i], 1), to_xn, 18)

        def last(i):
            wait((xs[i], yo, 0), 14 + i)
            if i == 3:
                arrived(buf.at[0:256, cut], sem_w.at[bank * 19 + 18])

        def left():
            gone(buf.at[0:1920, cut], 7 + bank)

        return start, early, late, last, left

    start_q, early_q, late_q, last_q, left_q = weights(gq, 0, 0, WIDE)
    start_o, early_o, late_o, last_o, left_o = weights(go, 1, 0, 512)
    start_g, early_g, late_g, last_g, left_g = weights(gf, 2, 0, 1024)
    start_d, early_d, late_d, last_d, left_d = weights(gf, 3, 1024, 512)

    def serve_start():
        theirs = pl.ds(pl.multiple_of((x * 4 + u * 2 + 1 - c) * 128, 128), 128)
        ours = pl.ds(pl.multiple_of(row * 128, 128), 128)

        @pl.when(source)
        def _():
            for i, (buf, srv) in enumerate(((gq, srvq), (go, srvo), (gf, srvf))):
                post(buf.at[theirs, :], srv, 11 + i, sem_own.at[i], to_core)
                srv[...] = buf[ours, :]

    def serve_end():
        @pl.when(jnp.logical_not(source))
        def _():
            for i, srv in enumerate((srvq, srvo, srvf)):
                arrived(srv, sem_own.at[i])

        store_weights()

    def stores():
        return [
            pltpu.make_async_copy(srvq, oq, loc_sem.at[7]),
            pltpu.make_async_copy(srvf.at[:, 0:512], of.at[0], loc_sem.at[8]),
            pltpu.make_async_copy(srvf.at[:, 512:1024], of.at[1], loc_sem.at[9]),
            pltpu.make_async_copy(turned.at[0], om_out, loc_sem.at[10]),
            pltpu.make_async_copy(turned.at[1], od_out, loc_sem.at[11]),
        ]

    def store_weights():
        turned[0] = jnp.transpose(srvo[...])
        turned[1] = jnp.transpose(srvf[:, 1024:1536])
        for one in stores():
            one.start()

    def scales(buf, first):
        @pl.loop(0, S // 128)
        def _(i):
            rows = pl.ds(pl.multiple_of(first + i * 128, 128), 128)
            tokens = buf[rows, :].astype(F32)
            total = jnp.sum(tokens * tokens, axis=1, keepdims=True)
            scl[rows, :] = jnp.broadcast_to(lax.rsqrt(total * (1.0 / D) + EPS), (128, 128))

    def project(i):
        feats = pl.ds(pl.multiple_of((x, xn, xp, xo)[i] * 512, 512), 512)

        @pl.loop(0, WIDE // 256)
        def _(n):
            wide = pl.ds(pl.multiple_of(n * 256, 256), 256)
            for m in range(REQS):
                rows = pl.ds(m * S, S)
                term = jnp.dot(xg[rows, feats], gq[feats, wide], preferred_element_type=F32)
                if i == 0:
                    acc[rows, wide] = term
                else:
                    acc[rows, wide] += term

    def retention(r):
        first = r * S
        rows = pl.ds(first, S)
        scale = scl[rows, :]
        for ref, at, gain in ((qs, 0, 1.0), (ks, KEY, 1.0 / math.sqrt(KEY))):
            a = (acc[rows, at : at + 128] * scale).astype(BF).astype(F32)
            b = (acc[rows, at + 128 : at + 256] * scale).astype(BF).astype(F32)
            ref[:, 0:128] = ((a * cosr[...] - b * sinr[...]) * gain).astype(BF)
            ref[:, 128:256] = ((a * sinr[...] + b * cosr[...]) * gain).astype(BF)
        wide_scale = jnp.concatenate([scale] * 4, axis=1)
        value = (acc[rows, 512:1024] * wide_scale).astype(BF)
        for t in range(S // BLOCK):
            q = qs[t * BLOCK : (t + 1) * BLOCK, :]
            total = jnp.zeros((BLOCK, VAL), F32)
            denom = jnp.zeros((BLOCK, 1), F32)
            for s in range(t + 1):
                k = ks[s * BLOCK : (s + 1) * BLOCK, :]
                score = lax.dot_general(q, k, NT, preferred_element_type=F32)
                score = score * (near[...] if s == t else far[...])
                denom += jnp.sum(score, axis=1, keepdims=True)
                total += jnp.dot(
                    score.astype(BF),
                    value[s * BLOCK : (s + 1) * BLOCK, :],
                    preferred_element_type=F32,
                )
            kept = total / jnp.maximum(jnp.abs(denom), 1.0)
            centred = kept - jnp.mean(kept, axis=1, keepdims=True)
            spread = jnp.mean(centred * centred, axis=1, keepdims=True)
            block = pl.ds(first + t * BLOCK, BLOCK)
            gate = (acc[block, 1024:1536] * wide_scale[t * BLOCK : (t + 1) * BLOCK, :]).astype(BF)
            mixed[block, :] = (
                jax.nn.silu(gate.astype(F32)) * (centred * lax.rsqrt(spread + EPS))
            ).astype(BF)

    def terms(left, weight, at, r, bank):
        rows = pl.ds(r * S, S)

        def term(slot):
            feats = pl.ds(pl.multiple_of(slot * FEAT, FEAT), FEAT)
            part[r, slot] = lax.dot_general(
                left[rows, :], weight[feats, at : at + 512], NT, preferred_element_type=F32
            ).astype(BF)

        @pl.loop(0, 4)
        def _(j):
            zz = lax.rem(zo + j, 4)
            slot = (1 - c) * 4 + zz
            term(slot)
            post(
                part.at[r, slot],
                pairs.at[bank, r, zz],
                14 + bank * 2 + r,
                sem_core.at[bank * 8 + r * 4 + zz],
                to_core,
            )

        @pl.loop(0, 4)
        def _(j):
            term(c * 4 + lax.rem(zo + j, 4))

    HALF = S // 2
    TOP, BOT = pl.ds(0, HALF), pl.ds(HALF, HALF)

    def pair(r, bank, zz):
        arrived(pairs.at[bank, r, zz], sem_core.at[bank * 8 + r * 4 + zz])
        slot = c * 4 + zz
        return slot

    def both(r, bank, zz, rows):
        return part[r, c * 4 + zz, rows, :].astype(F32) + pairs[bank, r, zz, rows, :].astype(F32)

    def reduce_start(r, bank):
        rel = (bank * 2 + r) * 2
        slot = pair(r, bank, zo)
        part[r, slot] = both(r, bank, zo, pl.ds(0, S)).astype(BF)
        post(part.at[r, slot, TOP, :], relay.at[bank, r, 0], 18 + bank * 2 + r, sem_rel.at[rel], to_zp)
        post(part.at[r, slot, BOT, :], relay.at[bank, r, 1], 18 + bank * 2 + r, sem_rel.at[rel + 1], to_zn)
        slot = pair(r, bank, zp)
        part[r, slot, BOT, :] = both(r, bank, zp, BOT).astype(BF)
        post(part.at[r, slot, BOT, :], final.at[bank, r, 0, BOT, :], 18 + bank * 2 + r, sem_fin.at[bank * 2 + r], to_zp)
        slot = pair(r, bank, zn)
        part[r, slot, TOP, :] = both(r, bank, zn, TOP).astype(BF)
        post(part.at[r, slot, TOP, :], final.at[bank, r, 1, TOP, :], 18 + bank * 2 + r, sem_fin.at[bank * 2 + r], to_zn)

    def reduce_relay(r, bank):
        rel = (bank * 2 + r) * 2
        arrived(relay.at[bank, r, 0], sem_rel.at[rel])
        slot = c * 4 + zp
        part[r, slot, TOP, :] = (both(r, bank, zp, TOP) + relay[bank, r, 0].astype(F32)).astype(BF)
        post(part.at[r, slot, TOP, :], final.at[bank, r, 0, TOP, :], 18 + bank * 2 + r, sem_fin.at[bank * 2 + r], to_zp)
        arrived(relay.at[bank, r, 1], sem_rel.at[rel + 1])
        slot = c * 4 + zn
        part[r, slot, BOT, :] = (both(r, bank, zn, BOT) + relay[bank, r, 1].astype(F32)).astype(BF)
        post(part.at[r, slot, BOT, :], final.at[bank, r, 1, BOT, :], 18 + bank * 2 + r, sem_fin.at[bank * 2 + r], to_zn)
        pair(r, bank, z)

    def reduce_end(r, bank):
        arrived(final.at[bank, r], sem_fin.at[bank * 2 + r])
        return (
            both(r, bank, z, pl.ds(0, S))
            + final[bank, r, 0].astype(F32)
            + final[bank, r, 1].astype(F32)
        )

    def reduce_gone(r, bank):
        gone(part.at[r, 0:4], 14 + bank * 2 + r)
        gone(part.at[r, 0:3], 18 + bank * 2 + r)

    def add_residual(r):
        rows = pl.ds(r * S, S)
        total = xg[rows, lanes(mine)].astype(F32) + reduce_end(r, 0)
        resid[rows, :] = total
        xm[rows, lanes(mine)] = total.astype(BF)

    def feed(r):
        rows = pl.ds(r * S, S)
        scales(xm, r * S)
        scale = jnp.concatenate([scl[rows, :]] * 2, axis=1)

        @pl.loop(0, 2)
        def _(n):
            at = pl.ds(pl.multiple_of(n * 256, 256), 256)
            up_at = pl.ds(pl.multiple_of(512 + n * 256, 256), 256)
            gate = jnp.dot(xm[rows, :], gf[:, at], preferred_element_type=F32) * scale
            up = jnp.dot(xm[rows, :], gf[:, up_at], preferred_element_type=F32) * scale
            hidden[rows, at] = (jax.nn.silu(gate) * up).astype(BF)

    def finish(r):
        rows = pl.ds(r * S, S)
        outb[rows, :] = (resid[rows, :] + reduce_end(r, 1)).astype(BF)

        @pl.when(jnp.logical_not(source))
        def _():
            post(outb.at[rows, :], swapb.at[rows, :], 22 + r, sem_swap.at[1 + r], to_swap)

    def save(r):
        rows = pl.ds(r * S, S)
        live = lax.broadcasted_iota(jnp.int32, (S, FEAT), 0) < lens[r]

        @pl.when(source)
        def _():
            swapb[rows, :] = jnp.where(live, outb[rows, :], jnp.zeros((S, FEAT), BF))

        @pl.when(jnp.logical_not(source))
        def _():
            arrived(swapb.at[rows, :], sem_swap.at[1 + r])
            swapb[rows, :] = jnp.where(live, swapb[rows, :], jnp.zeros((S, FEAT), BF))

        pltpu.make_async_copy(swapb.at[rows, :], y.at[rows, :], loc_sem.at[12 + r]).start()

    def saved(r):
        rows = pl.ds(r * S, S)
        pltpu.make_async_copy(swapb.at[rows, :], y.at[rows, :], loc_sem.at[12 + r]).wait()

    def out(r):
        terms(mixed, go, 0, r, 0)

    def down(r):
        reduce_gone(r, 0)
        terms(hidden, gf, 1024, r, 1)

    def act(step, r):
        step(xm, r * S, S, 1 + r)

    def deal_feed():
        for i in range(8):
            sbf[i, :, 0:512] = gm[0, :, i * 512 : (i + 1) * 512].astype(BF)
            sbf[i, :, 512:1024] = gm[1, :, i * 512 : (i + 1) * 512].astype(BF)
            sbf[i, :, 1024:1536] = dm[:, i * 512 : (i + 1) * 512].astype(BF)
        exchange(sbf, gf, 2, 0, 1536)

    def decays():
        head = c * 4 + z
        rate = jnp.float32(0.0)
        for i in range(HEADS):
            rate = jnp.where(head == i, jnp.float32(math.log1p(-(2.0 ** (-5 - i)))), rate)
        lag = lax.broadcasted_iota(jnp.int32, (BLOCK, BLOCK), 0) - lax.broadcasted_iota(
            jnp.int32, (BLOCK, BLOCK), 1
        )
        near[...] = jnp.where(lag >= 0, jnp.exp(jnp.maximum(lag, 0).astype(F32) * rate), 0.0)
        far[...] = jnp.exp((lag + BLOCK).astype(F32) * rate)

    exchanged(gq, 0, 0, WIDE)
    start_q()
    deal_feed()
    decays()
    end_swap()
    gather_start(xg, 0, TOK, 0)
    exchanged(go, 1, 0, 512)
    start_o()
    early_q(0)
    early_q(1)
    early_q(2)
    early_q(3)
    early_o(0)
    early_o(1)
    early_o(2)
    early_o(3)
    gather_near(xg, 0, TOK, 0)
    early_q(4)
    early_q(5)
    early_o(4)
    early_o(5)
    exchanged(gf, 2, 0, 1536)
    late_q(0)
    late_o(0)
    gather_far(xg, 0, TOK, 0)
    late_q(1)
    late_o(1)
    gather_core(xg, 0, TOK, 0)
    scales(xg, 0)
    late_q(2)
    late_o(2)
    scales(xg, S)
    late_q(3)
    late_o(3)
    start_g()
    last_q(0)
    project(0)
    last_q(1)
    project(1)
    last_q(2)
    project(2)
    last_q(3)
    project(3)
    early_g(0)
    early_g(1)
    retention(0)
    last_o(0)
    last_o(1)
    last_o(2)
    last_o(3)
    out(0)
    reduce_start(0, 0)
    early_g(2)
    early_g(3)
    early_g(4)
    early_g(5)
    start_d()
    retention(1)
    late_g(0)
    late_g(1)
    reduce_relay(0, 0)
    out(1)
    reduce_start(1, 0)
    late_g(2)
    late_g(3)
    early_d(0)
    early_d(1)
    early_d(2)
    early_d(3)
    add_residual(0)
    act(gather_start, 0)
    reduce_relay(1, 0)
    early_d(4)
    early_d(5)
    act(gather_near, 0)
    add_residual(1)
    act(gather_start, 1)
    late_d(0)
    late_d(1)
    act(gather_far, 0)
    act(gather_near, 1)
    late_d(2)
    late_d(3)
    act(gather_core, 0)
    last_g(0)
    last_g(1)
    last_g(2)
    last_g(3)
    feed(0)
    last_d(0)
    last_d(1)
    last_d(2)
    last_d(3)
    down(0)
    reduce_start(0, 1)
    act(gather_far, 1)
    act(gather_core, 1)
    feed(1)
    reduce_relay(0, 1)
    down(1)
    reduce_start(1, 1)
    finish(0)
    serve_start()
    reduce_relay(1, 1)
    save(0)
    serve_end()
    finish(1)
    save(1)

    for group, (buf, lo, width) in enumerate(((gq, 0, WIDE), (go, 0, 512), (gf, 0, 1536))):
        gone(buf.at[0:112, lo : lo + width], group)
    gather_gone(xg, 0, TOK, 0)
    for r in range(REQS):
        act(gather_gone, r)
        reduce_gone(r, 1)
    left_q()
    left_o()
    left_g()
    left_d()

    @pl.when(source)
    def _():
        for i, srv in enumerate((srvq, srvo, srvf)):
            gone(srv, 11 + i)

    @pl.when(jnp.logical_not(source))
    def _():
        gone(hid, 3)
        for r in range(REQS):
            gone(outb.at[pl.ds(r * S, S), :], 22 + r)

    for one in stores():
        one.wait()
    saved(0)
    saved(1)


def settle(y_in, q_in, f_in, m_in, d_in, y, q, f, m, d, yv, qv, fv, mv, dv, sem):
    sets = ((y_in, yv, y), (q_in, qv, q), (f_in, fv, f), (m_in, mv, m), (d_in, dv, d))
    takes = [pltpu.make_async_copy(a, b, sem.at[i]) for i, (a, b, _) in enumerate(sets)]
    gives = [pltpu.make_async_copy(b, c, sem.at[5 + i]) for i, (_, b, c) in enumerate(sets)]
    for one in takes:
        one.start()
    for one, two in zip(takes, gives):
        one.wait()
        two.start()
    for one in gives:
        one.wait()


def layer(lengths, hidden, qkvg, gateup, out_t, down_t):
    cosine, sine = tables()
    hbm = pl.BlockSpec(memory_space=pl.ANY)
    dma = pltpu.SemaphoreType.DMA
    shapes = (
        jax.ShapeDtypeStruct((TOK, FEAT), BF),
        jax.ShapeDtypeStruct((128, WIDE), BF),
        jax.ShapeDtypeStruct((2, 128, 512), BF),
        jax.ShapeDtypeStruct((512, 128), BF),
        jax.ShapeDtypeStruct((512, 128), BF),
    )
    scratch = [
        pltpu.VMEM((16, HEADS * WIDE), F32),
        pltpu.VMEM((2, 16, FF), F32),
        pltpu.VMEM((16, HEADS * VAL), F32),
        pltpu.VMEM((16, FF), F32),
        pltpu.VMEM((S, KEY // 2), F32),
        pltpu.VMEM((S, KEY // 2), F32),
        pltpu.VMEM((2, 512, 128), BF),
        pltpu.VMEM((8, 16, WIDE), BF),
        pltpu.VMEM((8, 16, 512), BF),
        pltpu.VMEM((8, 16, 1536), BF),
        pltpu.VMEM((128, WIDE), BF),
        pltpu.VMEM((128, 512), BF),
        pltpu.VMEM((128, 1536), BF),
        pltpu.VMEM((TOK, D), BF),
        pltpu.VMEM((TOK, D), BF),
        pltpu.VMEM((D, WIDE), BF),
        pltpu.VMEM((D, 512), BF),
        pltpu.VMEM((D, 1536), BF),
        pltpu.VMEM((TOK, WIDE), F32),
        pltpu.VMEM((TOK, 128), F32),
        pltpu.VMEM((BLOCK, BLOCK), F32),
        pltpu.VMEM((BLOCK, BLOCK), F32),
        pltpu.VMEM((S, KEY), BF),
        pltpu.VMEM((S, KEY), BF),
        pltpu.VMEM((TOK, VAL), BF),
        pltpu.VMEM((TOK, 512), BF),
        pltpu.VMEM((REQS, 8, S, FEAT), BF),
        pltpu.VMEM((2, REQS, 4, S, FEAT), BF),
        pltpu.VMEM((2, REQS, 2, S // 2, FEAT), BF),
        pltpu.VMEM((2, REQS, 2, S, FEAT), BF),
        pltpu.VMEM((TOK, FEAT), F32),
        pltpu.VMEM((TOK, FEAT), BF),
        pltpu.VMEM((TOK, FEAT), BF),
        dma((24,)),
        dma((3,)),
        dma((3,)),
        dma((76,)),
        dma((12,)),
        dma((16,)),
        dma((8,)),
        dma((4,)),
        dma((3,)),
        dma((14,)),
    ]
    results = pl.pallas_call(
        kernel,
        out_shape=shapes,
        in_specs=[pl.BlockSpec(memory_space=pltpu.SMEM)] + [hbm] * 7,
        out_specs=(hbm,) * 5,
        scratch_shapes=scratch,
        compiler_params=pltpu.CompilerParams(
            collective_id=0, has_side_effects=True, vmem_limit_bytes=62 * 1024 * 1024
        ),
    )(lengths, hidden, qkvg, gateup, out_t, down_t, jnp.asarray(cosine), jnp.asarray(sine))
    return pl.pallas_call(
        settle,
        out_shape=shapes,
        in_specs=[hbm] * 5,
        out_specs=(hbm,) * 5,
        scratch_shapes=[pltpu.VMEM(one.shape, one.dtype) for one in shapes] + [dma((10,))],
    )(*results)


def shards(hidden_states, lengths, qkvg_master, gateup_master, out_master, down_master):
    return layer(
        lengths, hidden_states, qkvg_master, gateup_master, out_master.T, down_master.T
    )


def solution(mesh):
    return jax.shard_map(
        shards,
        mesh=mesh,
        in_specs=(
            P("row", "col"),
            P("row"),
            P(("row", "col"), None),
            P(None, ("row", "col"), None),
            P(None, ("row", "col")),
            P(None, ("row", "col")),
        ),
        out_specs=(
            P("row", "col"),
            P("row", "col"),
            P(None, "row", "col"),
            P("col", "row"),
            P("col", "row"),
        ),
        check_vma=False,
    )
```
